32 devices in a mesh: tm: 8 (over z, y), slab: 4 (over x, core).
Axes of the slice: x: 2, y: 2, z: 4, core: 2. Of those that a mesh axis runs over, the one named last changes fastest.
Arguments:
- features: bfloat16 [8, 6144, 256], P('tm', 'slab'), may hold values from -6 to 6
- ref_lists: int32 [8, 4, 16], P('tm'), may hold values from 0 to 11
- tile_rows: int32 [8, 128], P('tm', 'slab'), may hold values from 0 to 11
- tile_sources: int32 [8, 128], P('tm', 'slab'), may hold values from 0 to 15
- tile_counts: int32 [8, 4], P('tm', 'slab'), may hold values from 9 to 32
- tile_values: bfloat16 [8, 128, 128, 128], P('tm', 'slab'), may hold values from -0.3125 to 0.3125
- w_input: bfloat16 [2, 256, 1024], replicated, may hold values from -0.375 to 0.375
- w_hidden: bfloat16 [2, 256, 1024], replicated, may hold values from -0.375 to 0.375
- bias: float32 [2, 1024], replicated, may hold values from -4 to 4
Outputs:
- hidden_out: bfloat16 [8, 6144, 256], P('tm', 'slab')
The draws below stay inside these ranges and needn't reach their ends.
Inputs may be any that keep to these rules, and one draw needn't show every extreme that they name: `ref_lists`: row tile indices within a slab. `tile_counts`: slots at or after the count are ignored.
All inputs are finite; a program needn't handle non-finite values.
Results may differ from the reference program's by a relative error of at most 0.0055.
Values may be sent and summed in bfloat16 or wider, within the bound.
No kernel may reach another device: no remote copies, remote signals or barrier semaphores. Data moves between devices by JAX's collectives and lax.ppermute only.
A program may use at most 64 MiB of HBM per device.

```python
import jax
import jax.numpy as jnp
from jax import lax

F = 256
H = 256
TILE = 128
ROWS = 1536
REFS = 4
LAYERS = 2
MAXT = 32
TIMES = 8
NODES = 6144
N_SLAB = 4


def place_ends(result, rng, least, top_value):
    dims = result.shape
    spot = [jax.random.randint(jax.random.fold_in(rng, axis), (), 0, dims[axis]) for axis in range(len(dims))]
    result = result.at[tuple(spot)].set(least)
    longest = dims.index(max(dims))
    spot[longest] = (spot[longest] + 1) % dims[longest]
    return result.at[tuple(spot)].set(top_value)


def block_levels(stream_key, extent, pieces, low, high):
    level = 1.0
    for axis_at, parts in pieces:
        steps = jax.random.uniform(jax.random.fold_in(jax.random.fold_in(stream_key, 6), axis_at), (parts,), jnp.float32, low / len(pieces), high / len(pieces))
        level = level * jnp.repeat(jnp.exp(steps), extent[axis_at] // parts).reshape((-1,) + (1,) * (len(extent) - 1 - axis_at))
    return level


def gaussian(own_key, shape, width, limit, pieces=(), kind=jnp.bfloat16):
    drawn = jax.random.normal(own_key, shape, jnp.float32) * width
    if len(pieces) > 0:
        drawn = block_levels(own_key, shape, pieces, -0.22, 0.18) * drawn
    return jnp.clip(drawn, min=-limit, max=limit).astype(kind)


def setup_inputs(seed: int = 0) -> dict:
    seeds = jax.random.split(jax.random.key(seed), 10)
    features = gaussian(seeds[0], (TIMES, NODES, F), 1.0, 6.0, ((0, 8), (1, 4)))
    ref_lists = place_ends(jax.random.randint(seeds[1], (TIMES, N_SLAB, N_SLAB * REFS), 0, ROWS // TILE), jax.random.fold_in(seeds[1], 1), 0, (ROWS // TILE) - 1).astype(jnp.int32)
    tile_rows = place_ends(jax.random.randint(seeds[2], (TIMES, N_SLAB * MAXT), 0, ROWS // TILE), jax.random.fold_in(seeds[2], 1), 0, (ROWS // TILE) - 1).astype(jnp.int32)
    tile_sources = place_ends(jax.random.randint(seeds[3], (TIMES, N_SLAB * MAXT), 0, N_SLAB * REFS), jax.random.fold_in(seeds[3], 1), 0, (N_SLAB * REFS) - 1).astype(jnp.int32)
    tile_counts = place_ends(jax.random.randint(seeds[4], (TIMES, N_SLAB), MAXT // 4 + 1, MAXT + 1), jax.random.fold_in(seeds[4], 1), MAXT // 4 + 1, MAXT).astype(jnp.int32)
    tile_values = gaussian(seeds[5], (TIMES, N_SLAB * MAXT, TILE, TILE), (3 * TILE) ** -0.5, 0.3125, ((0, 8), (1, 4)))
    w_input = gaussian(seeds[6], (LAYERS, F, 4 * H), F ** -0.5, 0.375)
    w_hidden = gaussian(seeds[7], (LAYERS, H, 4 * H), H ** -0.5, 0.375)
    bias = gaussian(seeds[8], (LAYERS, 4 * H), 1.0, 4.0, (), jnp.float32)
    return {"features": features, "ref_lists": ref_lists, "tile_rows": tile_rows, "tile_sources": tile_sources, "tile_counts": tile_counts, "tile_values": tile_values, "w_input": w_input, "w_hidden": w_hidden, "bias": bias}


def lstm_run(inputs, weight_in, weight_rec, gate_bias):
    steps_count, vertex_count, feature_width = inputs.shape
    projected = jnp.dot(inputs.reshape(-1, feature_width), weight_in, preferred_element_type=jnp.float32)
    projected = projected.reshape(steps_count, vertex_count, -1) + gate_bias
    unit_count = weight_rec.shape[0]

    def advance(state, gate_input):
        hidden, memory = state
        gate_sum = gate_input + jnp.dot(hidden, weight_rec, preferred_element_type=jnp.float32)
        in_gate, forget, candidate, out_gate = jnp.split(gate_sum, 4, axis=-1)
        memory = jax.nn.sigmoid(forget) * memory + jax.nn.sigmoid(in_gate) * jnp.tanh(candidate)
        hidden = (jax.nn.sigmoid(out_gate) * jnp.tanh(memory)).astype(jnp.bfloat16)
        return (hidden, memory), hidden

    start_state = (jnp.zeros((vertex_count, unit_count), jnp.bfloat16), jnp.zeros((vertex_count, unit_count), jnp.float32))
    final_state, outputs = lax.scan(advance, start_state, projected, unroll=4)
    return outputs


def convolve(snapshot):
    current, ref_table, row_list, source_list, count_list, weight_tiles = snapshot
    row_tiles = ROWS // TILE
    tiles = current.reshape(N_SLAB * row_tiles, TILE, -1)
    offsets = jnp.arange(N_SLAB * REFS, dtype=jnp.int32) // REFS * row_tiles
    global_table = ref_table + offsets[None, :]
    sources = source_list.reshape(N_SLAB, MAXT)
    global_index = jnp.take_along_axis(global_table, sources, axis=1)
    picked = jnp.take(tiles, global_index.reshape(-1), axis=0).reshape(N_SLAB, MAXT, TILE, -1)
    weights = weight_tiles.reshape(N_SLAB, MAXT, TILE, TILE)
    products = jnp.einsum("pkij,pkjf->pkif", weights.astype(jnp.float32), picked.astype(jnp.float32))
    live = jnp.arange(MAXT, dtype=jnp.int32)[None, :] < count_list[:, None]
    targets = row_list.reshape(N_SLAB, MAXT)
    one_hot = (targets[:, None, :] == jnp.arange(row_tiles, dtype=jnp.int32)[None, :, None]) & live[:, None, :]
    mixed = jnp.einsum("prk,pkif->prif", one_hot.astype(jnp.float32), products)
    return mixed.reshape(NODES, -1).astype(jnp.bfloat16)


def reference(features, ref_lists, tile_rows, tile_sources, tile_counts, tile_values, w_input, w_hidden, bias):
    current = features
    for layer_index in range(LAYERS):
        mixed = lax.map(convolve, (current, ref_lists, tile_rows, tile_sources, tile_counts, tile_values))
        blocks = mixed.reshape(TIMES, N_SLAB, ROWS, -1).transpose(1, 0, 2, 3)

        def run_block(block_rows):
            return lstm_run(block_rows, w_input[layer_index], w_hidden[layer_index], bias[layer_index])

        states = lax.map(run_block, blocks)
        current = states.transpose(1, 0, 2, 3).reshape(TIMES, NODES, -1)
    return current
```

```python
import jax
import jax.numpy as jnp
from jax import lax
from jax.experimental import pallas as pl
from jax.experimental.pallas import tpu as pltpu
from jax.sharding import PartitionSpec as P


ANY = pl.BlockSpec(memory_space=pl.ANY)
SMEM = pl.BlockSpec(memory_space=pltpu.SMEM)
VMEM = pl.BlockSpec(memory_space=pltpu.VMEM)
UNROLL = 4


def run_all(copies):
    for copy in copies:
        copy.start()
    for copy in copies:
        copy.wait()


def pick_tiles(parts, ref_table, slab_count, row_count, tile):
    part_count = len(parts)
    part_rows, width = parts[0].shape
    listed = ref_table.shape[2] // slab_count

    def kernel(table, *refs):
        sources = refs[:part_count]
        outs = refs[part_count : part_count + slab_count]
        rows, part_sems, tile_sems = refs[part_count + slab_count :]
        slab = lax.axis_index("slab")
        place = lax.axis_index("tm") % part_count
        run_all(
            [
                pltpu.make_async_copy(
                    sources[k],
                    rows.at[pl.ds(pl.multiple_of((place ^ k) * part_rows, part_rows), part_rows)],
                    part_sems.at[k],
                )
                for k in range(part_count)
            ]
        )
        copies = []
        for k in range(slab_count):
            for j in range(listed):
                index = table[0, slab ^ k, slab * listed + j]
                copies.append(
                    pltpu.make_async_copy(
                        rows.at[pl.ds(pl.multiple_of(index * tile, tile), tile)],
                        outs[k].at[pl.ds(j * tile, tile)],
                        tile_sems.at[k, j],
                    )
                )
        run_all(copies)

    return pl.pallas_call(
        kernel,
        in_specs=[SMEM] + [ANY] * part_count,
        out_specs=[ANY] * slab_count,
        out_shape=[jax.ShapeDtypeStruct((listed * tile, width), parts[0].dtype)] * slab_count,
        scratch_shapes=[
            pltpu.VMEM((row_count, width), parts[0].dtype),
            pltpu.SemaphoreType.DMA((part_count,)),
            pltpu.SemaphoreType.DMA((slab_count, listed)),
        ],
        name="pick_tiles",
    )(ref_table, *parts)


def convolve(arrived, tile_rows, tile_sources, tile_counts, tile_values, row_count, group):
    slab_count = len(arrived)
    piece, width = arrived[0].shape
    slots, tile = tile_values.shape[1:3]
    group_rows = row_count // group

    def kernel(rows, sources, counts, values_hbm, *refs):
        pieces = refs[:slab_count]
        outs = refs[slab_count : slab_count + group]
        values, inputs, total, mixed, in_sems, out_sems = refs[slab_count + group :]
        slab = lax.axis_index("slab")
        place = lax.axis_index("tm") % group
        copies = [pltpu.make_async_copy(values_hbm.at[0], values, in_sems.at[slab_count])]
        for k in range(slab_count):
            start = pl.multiple_of((slab ^ k) * piece, piece)
            copies.append(
                pltpu.make_async_copy(pieces[k], inputs.at[pl.ds(start, piece)], in_sems.at[k])
            )
        for copy in copies:
            copy.start()
        total[...] = jnp.zeros_like(total)
        for copy in copies:
            copy.wait()
        count = counts[0, 0]

        def step(index, carry):
            products = []
            for lane in range(UNROLL):
                slot = index * UNROLL + lane
                start = pl.multiple_of(sources[0, slot] * tile, tile)
                product = jnp.dot(
                    values[slot],
                    inputs[pl.ds(start, tile), :],
                    preferred_element_type=jnp.float32,
                )
                products.append(jnp.where(slot < count, product, 0.0))
            for lane in range(UNROLL):
                target = pl.multiple_of(rows[0, index * UNROLL + lane] * tile, tile)
                total[pl.ds(target, tile), :] += products[lane]
            return carry

        lax.fori_loop(0, (count + UNROLL - 1) // UNROLL, step, 0)
        mixed[...] = total[...].astype(mixed.dtype)
        run_all(
            [
                pltpu.make_async_copy(
                    mixed.at[
                        pl.ds(pl.multiple_of((place ^ k) * group_rows, group_rows), group_rows)
                    ],
                    outs[k],
                    out_sems.at[k],
                )
                for k in range(group)
            ]
        )

    dtype = arrived[0].dtype
    return pl.pallas_call(
        kernel,
        in_specs=[SMEM, SMEM, SMEM, ANY] + [ANY] * slab_count,
        out_specs=[ANY] * group,
        out_shape=[jax.ShapeDtypeStruct((group_rows, width), dtype)] * group,
        scratch_shapes=[
            pltpu.VMEM((slots, tile, tile), tile_values.dtype),
            pltpu.VMEM((slab_count * piece, width), dtype),
            pltpu.VMEM((row_count, width), jnp.float32),
            pltpu.VMEM((row_count, width), dtype),
            pltpu.SemaphoreType.DMA((slab_count + 1,)),
            pltpu.SemaphoreType.DMA((group,)),
        ],
        name="convolve",
    )(tile_rows, tile_sources, tile_counts, tile_values, *arrived)


def sigmoid(value):
    return 0.5 * jnp.tanh(0.5 * value) + 0.5


def recur(mixed, layer, w_input, w_hidden, bias):
    group = len(mixed)
    rows, width = mixed[0].shape
    units = w_hidden.shape[1]

    def kernel(w_in, w_rec, gate_bias, *refs):
        sources = refs[:group]
        outs = refs[group : 2 * group]
        inputs, states, memory, in_sems, out_sems = refs[2 * group :]
        place = lax.axis_index("tm") % group
        run_all(
            [
                pltpu.make_async_copy(sources[k], inputs.at[place ^ k], in_sems.at[k])
                for k in range(group)
            ]
        )
        line = gate_bias[pl.ds(layer, 1), :]

        def advance(gates, old, time):
            i, f, g, o = (gates[:, n * units : (n + 1) * units] for n in range(4))
            new = sigmoid(i) * jnp.tanh(g)
            if old is not None:
                new = sigmoid(f) * old + new
            memory[...] = new
            states[time] = (sigmoid(o) * jnp.tanh(new)).astype(states.dtype)

        def project(time):
            return jnp.dot(inputs[time], w_in[layer], preferred_element_type=jnp.float32) + line

        advance(project(0), None, 0)

        def step(time, carry):
            gates = project(time) + jnp.dot(
                states[time - 1], w_rec[layer], preferred_element_type=jnp.float32
            )
            advance(gates, memory[...], time)
            return carry

        lax.fori_loop(1, group, step, 0)
        run_all(
            [
                pltpu.make_async_copy(states.at[place ^ k], outs[k], out_sems.at[k])
                for k in range(group)
            ]
        )

    dtype = mixed[0].dtype
    return pl.pallas_call(
        kernel,
        in_specs=[VMEM, VMEM, VMEM] + [ANY] * group,
        out_specs=[ANY] * group,
        out_shape=[jax.ShapeDtypeStruct((rows, units), dtype)] * group,
        scratch_shapes=[
            pltpu.VMEM((group, rows, width), dtype),
            pltpu.VMEM((group, rows, units), dtype),
            pltpu.VMEM((rows, units), jnp.float32),
            pltpu.SemaphoreType.DMA((group,)),
            pltpu.SemaphoreType.DMA((group,)),
        ],
        name="recur",
    )(w_input, w_hidden, bias, *mixed)


def assemble(parts):
    part_count = len(parts)
    part_rows, width = parts[0].shape

    def kernel(*refs):
        out, sems = refs[part_count:]
        place = lax.axis_index("tm") % part_count
        run_all(
            [
                pltpu.make_async_copy(
                    refs[k],
                    out.at[0, pl.ds(pl.multiple_of((place ^ k) * part_rows, part_rows), part_rows)],
                    sems.at[k],
                )
                for k in range(part_count)
            ]
        )

    return pl.pallas_call(
        kernel,
        in_specs=[ANY] * part_count,
        out_specs=ANY,
        out_shape=jax.ShapeDtypeStruct((1, part_count * part_rows, width), parts[0].dtype),
        scratch_shapes=[pltpu.SemaphoreType.DMA((part_count,))],
        name="assemble",
    )(*parts)


def swap(arrays, axis, order):
    count = lax.axis_size(axis)
    got = list(arrays)
    for k in order:
        got[k] = lax.ppermute(arrays[k], axis, [(n, n ^ k) for n in range(count)])
    return got


def local(
    features, ref_lists, tile_rows, tile_sources, tile_counts, tile_values, w_input, w_hidden, bias
):
    row_count = features.shape[1]
    tile = tile_values.shape[2]
    slab_count = lax.axis_size("slab")
    group = lax.axis_size("tm")
    far_slab = range(slab_count - 1, 0, -1)
    far_time = range(group - 1, 0, -1)
    parts = [features[0]]
    for layer in range(w_input.shape[0]):
        listed = pick_tiles(parts, ref_lists, slab_count, row_count, tile)
        arrived = swap(listed, "slab", far_slab)
        mixed = convolve(
            arrived, tile_rows, tile_sources, tile_counts, tile_values, row_count, group
        )
        mixed = swap(mixed, "tm", far_time)
        parts = swap(recur(mixed, layer, w_input, w_hidden, bias), "tm", far_time)
    return assemble(parts)


def solution(mesh):
    in_specs = (
        P("tm", "slab", None),
        P("tm", None, None),
        P("tm", "slab"),
        P("tm", "slab"),
        P("tm", "slab"),
        P("tm", "slab", None, None),
        P(),
        P(),
        P(),
    )
    out_specs = P("tm", "slab", None)
    return jax.shard_map(local, mesh=mesh, in_specs=in_specs, out_specs=out_specs, check_vma=False)
```

```python
import jax
import jax.numpy as jnp
from jax import lax
from jax.experimental import pallas as pl
from jax.experimental.pallas import tpu as pltpu
from jax.sharding import PartitionSpec as P


ANY = pl.BlockSpec(memory_space=pl.ANY)
SMEM = pl.BlockSpec(memory_space=pltpu.SMEM)
VMEM = pl.BlockSpec(memory_space=pltpu.VMEM)
PARAMS = pltpu.CompilerParams(vmem_limit_bytes=24 * 2**20)
UNROLL = 4
AXES = ("tm", "slab")
LOWER, UPPER, BOTH = 0, 1, None


def seat(group):
    index = lax.axis_index("tm")
    half = index // group
    place = index % group
    return half, place, place ^ (half * mirror(group))


def mirror(group):
    return group - 2 if group > 2 else 0


def only(mode, half):
    def run(body):
        if mode is BOTH:
            body()
        else:
            pl.when(half == mode)(body)

    return run


def pick_tiles(parts, ref_table, slab_count, row_count, tile, group, mode):
    part_count = len(parts)
    part_rows, width = parts[0].shape
    listed = ref_table.shape[2] // slab_count

    def kernel(table, *refs):
        sources = refs[:part_count]
        outs = refs[part_count : part_count + slab_count]
        slab = lax.axis_index("slab")
        half, _, lead = seat(group)

        @only(mode, half)
        def _():
            rows = sources[0]
            if part_count > 1:
                rows = refs[-1]
                for k in range(part_count):
                    start = pl.multiple_of((lead ^ k) * part_rows, part_rows)
                    rows[pl.ds(start, part_rows), :] = sources[k][...]
            for k in reversed(range(slab_count)):
                for j in range(listed):
                    index = table[0, slab ^ k, slab * listed + j]
                    start = pl.multiple_of(index * tile, tile)
                    outs[k][j * tile : (j + 1) * tile, :] = rows[pl.ds(start, tile), :]

    dtype = parts[0].dtype
    return pl.pallas_call(
        kernel,
        in_specs=[SMEM] + [VMEM] * part_count,
        out_specs=[VMEM] * slab_count,
        out_shape=[jax.ShapeDtypeStruct((listed * tile, width), dtype)] * slab_count,
        scratch_shapes=[pltpu.VMEM((row_count, width), dtype)] if part_count > 1 else [],
        compiler_params=PARAMS,
        name="pick_tiles",
    )(ref_table, *parts)


def convolve(arrived, tile_rows, tile_sources, tile_counts, tile_values, row_count, group, mode):
    slab_count = len(arrived)
    piece, width = arrived[0].shape
    tile = tile_values.shape[2]
    group_rows = row_count // group

    def kernel(rows, sources, counts, values, *refs):
        pieces = refs[:slab_count]
        outs = refs[slab_count : slab_count + group]
        inputs, total = refs[slab_count + group :]
        slab = lax.axis_index("slab")
        half, _, lead = seat(group)

        @only(mode, half)
        def _():
            for k in range(slab_count):
                start = pl.multiple_of((slab ^ k) * piece, piece)
                inputs[pl.ds(start, piece), :] = pieces[k][...]
            total[...] = jnp.zeros_like(total)
            count = counts[0, 0]

            def step(index, carry):
                products = []
                for lane in range(UNROLL):
                    slot = index * UNROLL + lane
                    start = pl.multiple_of(sources[0, slot] * tile, tile)
                    product = jnp.dot(
                        values[0, slot],
                        inputs[pl.ds(start, tile), :],
                        preferred_element_type=jnp.float32,
                    )
                    products.append(jnp.where(slot < count, product, 0.0))
                for lane in range(UNROLL):
                    target = pl.multiple_of(rows[0, index * UNROLL + lane] * tile, tile)
                    total[pl.ds(target, tile), :] += products[lane]
                return carry

            lax.fori_loop(0, (count + UNROLL - 1) // UNROLL, step, 0)
            for k in range(group):
                start = pl.multiple_of((lead ^ k) * group_rows, group_rows)
                outs[k][...] = total[pl.ds(start, group_rows), :].astype(outs[k].dtype)

    dtype = arrived[0].dtype
    return pl.pallas_call(
        kernel,
        in_specs=[SMEM, SMEM, SMEM, VMEM] + [VMEM] * slab_count,
        out_specs=[VMEM] * group,
        out_shape=[jax.ShapeDtypeStruct((group_rows, width), dtype)] * group,
        scratch_shapes=[
            pltpu.VMEM((slab_count * piece, width), dtype),
            pltpu.VMEM((row_count, width), jnp.float32),
        ],
        compiler_params=PARAMS,
        name="convolve",
    )(tile_rows, tile_sources, tile_counts, tile_values, *arrived)


def sigmoid(value):
    return 0.5 * jnp.tanh(0.5 * value) + 0.5


def recur(mixed, layer, w_input, w_hidden, bias, mode, state=None, after=None):
    group = len(mixed)
    rows, width = mixed[0].shape
    units = w_hidden.shape[1]
    extra = [value for value in (state, after) if value is not None]
    first = group + len(extra)

    def kernel(w_in, w_rec, gate_bias, *refs):
        sources = refs[:group]
        outs = refs[first : first + group]
        last, token = refs[first + group : first + group + 2]
        inputs, states, memory = refs[first + group + 2 :]
        half, place, _ = seat(group)

        @only(mode, half)
        def _():
            for k in range(group):
                inputs[place ^ k] = sources[k][...]
            line = gate_bias[layer : layer + 1, :]

            def advance(gates, old, time):
                i, f, g, o = (gates[:, n * units : (n + 1) * units] for n in range(4))
                new = sigmoid(i) * jnp.tanh(g)
                if old is not None:
                    new = sigmoid(f) * old + new
                memory[...] = new
                states[time] = (sigmoid(o) * jnp.tanh(new)).astype(states.dtype)

            def project(time):
                return jnp.dot(inputs[time], w_in[layer], preferred_element_type=jnp.float32) + line

            def step(time, carry):
                gates = project(time) + jnp.dot(
                    carry, w_rec[layer], preferred_element_type=jnp.float32
                )
                advance(gates, memory[...], time)
                return states[time]

            if state is None:
                advance(project(0), None, 0)
            else:
                memory[...] = refs[group][1].astype(jnp.float32)
                step(0, refs[group][0])

            def loop(time, carry):
                step(time, states[time - 1])
                return carry

            lax.fori_loop(1, group, loop, 0)
            for k in range(group):
                outs[k][...] = states[place ^ k]
            last[0] = states[group - 1]
            last[1] = memory[...].astype(last.dtype)

        token[...] = jnp.zeros_like(token)

    dtype = mixed[0].dtype
    *hidden, last, token = pl.pallas_call(
        kernel,
        in_specs=[VMEM] * (3 + first),
        out_specs=[VMEM] * (group + 2),
        out_shape=[jax.ShapeDtypeStruct((rows, units), dtype)] * group
        + [
            jax.ShapeDtypeStruct((2, rows, units), dtype),
            jax.ShapeDtypeStruct((8, 128), jnp.float32),
        ],
        scratch_shapes=[
            pltpu.VMEM((group, rows, width), dtype),
            pltpu.VMEM((group, rows, units), dtype),
            pltpu.VMEM((rows, units), jnp.float32),
        ],
        compiler_params=PARAMS,
        name="recur",
    )(w_input, w_hidden, bias, *mixed, *extra)
    return hidden, last, token


def assemble(lists, group):
    part_rows, width = lists[0][0].shape

    def kernel(*refs):
        out, sems = refs[-2:]
        half, _, lead = seat(group)
        for mode in range(len(lists)):

            @only(mode, half)
            def _():
                copies = []
                for k in range(group):
                    start = pl.multiple_of((lead ^ k) * part_rows, part_rows)
                    copies.append(
                        pltpu.make_async_copy(
                            refs[mode * group + k], out.at[0, pl.ds(start, part_rows)], sems.at[k]
                        )
                    )
                for copy in copies:
                    copy.start()
                for copy in copies:
                    copy.wait()

    parts = [part for parts in lists for part in parts]
    return pl.pallas_call(
        kernel,
        in_specs=[VMEM] * len(parts),
        out_specs=ANY,
        out_shape=jax.ShapeDtypeStruct((1, group * part_rows, width), parts[0].dtype),
        scratch_shapes=[pltpu.SemaphoreType.DMA((group,))],
        compiler_params=PARAMS,
        name="assemble",
    )(*parts)


def send(array, group, mode, target):
    slab_count = lax.axis_size("slab")
    pairs = []
    for time in range(lax.axis_size("tm")):
        if mode is BOTH or time // group == mode:
            for slab in range(slab_count):
                to_time, to_slab = target(time, slab)
                pairs.append((time * slab_count + slab, to_time * slab_count + to_slab))
    return lax.ppermute(array, AXES, pairs)


def swap_slabs(arrays, group, mode):
    got = list(arrays)
    for k in range(len(arrays) - 1, 0, -1):
        got[k] = send(arrays[k], group, mode, lambda time, slab: (time, slab ^ k))
    return got


def swap_times(arrays, group, mode):
    got = list(arrays)
    for k in range(len(arrays) - 1, 0, -1):
        got[k] = send(arrays[k], group, mode, lambda time, slab: (time ^ k, slab))
    return got


def hand_over(last, group):
    return send(
        last, group, LOWER, lambda time, slab: (group + (time ^ mirror(group)), slab)
    )


def local(
    features, ref_lists, tile_rows, tile_sources, tile_counts, tile_values, w_input, w_hidden, bias
):
    row_count = features.shape[1]
    tile = tile_values.shape[2]
    slab_count = lax.axis_size("slab")
    layers = w_input.shape[0]
    group = lax.axis_size("tm") // 2

    def mix(parts, mode):
        listed = pick_tiles(parts, ref_lists, slab_count, row_count, tile, group, mode)
        arrived = swap_slabs(listed, group, mode)
        mixed = convolve(
            arrived, tile_rows, tile_sources, tile_counts, tile_values, row_count, group, mode
        )
        return swap_times(mixed, group, mode)

    def run(mixed, layer, mode, state=None, after=None):
        return recur(mixed, layer, w_input, w_hidden, bias, mode, state, after)

    mixed = mix([features[0]], BOTH)
    lower_mixed, upper_mixed = mixed, mixed
    handed, token = [], None
    for layer in range(layers + 1):
        if layer < layers:
            hidden, last, token = run(lower_mixed, layer, LOWER)
            handed.append(hand_over(last, group))
            lower = swap_times(hidden, group, LOWER)
            if layer + 1 < layers:
                lower_mixed = mix(lower, LOWER)
        if layer > 0:
            hidden, _, _ = run(upper_mixed, layer - 1, UPPER, handed[layer - 1], token)
            upper = swap_times(hidden, group, UPPER)
            if layer < layers:
                upper_mixed = mix(upper, UPPER)
    return assemble([lower, upper], group)


def solution(mesh):
    in_specs = (
        P("tm", "slab", None),
        P("tm", None, None),
        P("tm", "slab"),
        P("tm", "slab"),
        P("tm", "slab"),
        P("tm", "slab", None, None),
        P(),
        P(),
        P(),
    )
    out_specs = P("tm", "slab", None)
    return jax.shard_map(local, mesh=mesh, in_specs=in_specs, out_specs=out_specs, check_vma=False)
```

```python
import jax
import jax.numpy as jnp
from jax import lax
from jax.experimental import pallas as pl
from jax.experimental.pallas import tpu as pltpu
from jax.sharding import PartitionSpec as P


ANY = pl.BlockSpec(memory_space=pl.ANY)
SMEM = pl.BlockSpec(memory_space=pltpu.SMEM)
VMEM = pl.BlockSpec(memory_space=pltpu.VMEM)
PARAMS = pltpu.CompilerParams(vmem_limit_bytes=24 * 2**20)
UNROLL = 4
AXES = ("tm", "slab")
LOWER, UPPER, BOTH = 0, 1, None


def seat(group):
    index = lax.axis_index("tm")
    half = index // group
    place = index % group
    return half, place, place ^ (half * mirror(group))


def mirror(group):
    return group - 2 if group > 2 else 0


def only(mode, half):
    def run(body):
        if mode is BOTH:
            body()
        else:
            pl.when(half == mode)(body)

    return run


def pick_tiles(parts, ref_table, slab_count, row_count, tile, group, mode):
    part_count = len(parts)
    part_rows, width = parts[0].shape
    listed = ref_table.shape[2] // slab_count

    def kernel(table, *refs):
        sources = refs[:part_count]
        outs = refs[part_count : part_count + slab_count]
        slab = lax.axis_index("slab")
        half, place, lead = seat(group)

        @only(mode, half)
        def _():
            rows = sources[0]
            if part_count > 1:
                rows = refs[-1]
                for k in range(part_count):
                    start = pl.multiple_of((lead ^ k) * part_rows, part_rows)
                    rows[pl.ds(start, part_rows), :] = sources[k][...]
            for k in reversed(range(slab_count)):
                for j in range(listed):
                    index = table[0, slab ^ k, slab * listed + j]
                    start = pl.multiple_of(index * tile, tile)
                    outs[k][j * tile : (j + 1) * tile, :] = rows[pl.ds(start, tile), :]

    dtype = parts[0].dtype
    return pl.pallas_call(
        kernel,
        in_specs=[SMEM] + [VMEM] * part_count,
        out_specs=[VMEM] * slab_count,
        out_shape=[jax.ShapeDtypeStruct((listed * tile, width), dtype)] * slab_count,
        scratch_shapes=[pltpu.VMEM((row_count, width), dtype)] if part_count > 1 else [],
        compiler_params=PARAMS,
        name="pick_tiles",
    )(ref_table, *parts)


def convolve(arrived, tile_rows, tile_sources, tile_counts, tile_values, row_count, group, mode):
    slab_count = len(arrived)
    piece, width = arrived[0].shape
    tile = tile_values.shape[2]
    group_rows = row_count // group

    def kernel(rows, sources, counts, values, *refs):
        pieces = refs[:slab_count]
        outs = refs[slab_count : slab_count + group]
        inputs, total = refs[slab_count + group :]
        slab = lax.axis_index("slab")
        half, place, lead = seat(group)

        @only(mode, half)
        def _():
            for k in range(slab_count):
                start = pl.multiple_of((slab ^ k) * piece, piece)
                inputs[pl.ds(start, piece), :] = pieces[k][...]
            total[...] = jnp.zeros_like(total)
            count = counts[0, 0]

            def step(index, carry):
                products = []
                for lane in range(UNROLL):
                    slot = index * UNROLL + lane
                    start = pl.multiple_of(sources[0, slot] * tile, tile)
                    product = jnp.dot(
                        values[0, slot],
                        inputs[pl.ds(start, tile), :],
                        preferred_element_type=jnp.float32,
                    )
                    products.append(jnp.where(slot < count, product, 0.0))
                for lane in range(UNROLL):
                    target = pl.multiple_of(rows[0, index * UNROLL + lane] * tile, tile)
                    total[pl.ds(target, tile), :] += products[lane]
                return carry

            lax.fori_loop(0, (count + UNROLL - 1) // UNROLL, step, 0)
            for k in range(group):
                start = pl.multiple_of((lead ^ k) * group_rows, group_rows)
                outs[k][...] = total[pl.ds(start, group_rows), :].astype(outs[k].dtype)

    dtype = arrived[0].dtype
    return pl.pallas_call(
        kernel,
        in_specs=[SMEM, SMEM, SMEM, VMEM] + [VMEM] * slab_count,
        out_specs=[VMEM] * group,
        out_shape=[jax.ShapeDtypeStruct((group_rows, width), dtype)] * group,
        scratch_shapes=[
            pltpu.VMEM((slab_count * piece, width), dtype),
            pltpu.VMEM((row_count, width), jnp.float32),
        ],
        compiler_params=PARAMS,
        name="convolve",
    )(tile_rows, tile_sources, tile_counts, tile_values, *arrived)


def sigmoid(value):
    return 0.5 * jnp.tanh(0.5 * value) + 0.5


def recur(mixed, layer, w_input, w_hidden, bias, mode, state=None, keep=()):
    group = len(mixed)
    rows, width = mixed[0].shape
    units = w_hidden.shape[1]
    first = state is None
    operands = list(mixed) + list(keep) + ([] if first else [state])

    def kernel(w_in, w_rec, gate_bias, *refs):
        sources = refs[:group]
        kept = refs[group : group + len(keep)]
        start = refs[len(operands) - 1]
        outs = refs[len(operands) : len(operands) + group]
        inputs, states, memory = refs[-3:]
        half, place, lead = seat(group)

        if keep:

            @pl.when(half != mode)
            def _():
                for k in range(group):
                    outs[k][...] = kept[k][...]

        @only(mode, half)
        def _():
            for k in range(group):
                inputs[place ^ k] = sources[k][...]
            line = gate_bias[layer : layer + 1, :]

            def advance(gates, old, time):
                i, f, g, o = (gates[:, n * units : (n + 1) * units] for n in range(4))
                new = sigmoid(i) * jnp.tanh(g)
                if old is not None:
                    new = sigmoid(f) * old + new
                memory[...] = new
                states[time] = (sigmoid(o) * jnp.tanh(new)).astype(states.dtype)

            def project(time):
                return jnp.dot(inputs[time], w_in[layer], preferred_element_type=jnp.float32) + line

            def step(time, carry):
                gates = project(time) + jnp.dot(
                    carry, w_rec[layer], preferred_element_type=jnp.float32
                )
                advance(gates, memory[...], time)
                return states[time]

            if first:
                advance(project(0), None, 0)
            else:
                memory[...] = start[1].astype(jnp.float32)
                step(0, start[0])

            def loop(time, carry):
                step(time, states[time - 1])
                return carry

            lax.fori_loop(1, group, loop, 0)
            for k in range(group):
                outs[k][...] = states[place ^ k]
            if first:
                last = refs[len(operands) + group]
                last[0] = states[group - 1]
                last[1] = memory[...].astype(last.dtype)

    dtype = mixed[0].dtype
    out_shape = [jax.ShapeDtypeStruct((rows, units), dtype)] * group
    if first:
        out_shape.append(jax.ShapeDtypeStruct((2, rows, units), dtype))
    return pl.pallas_call(
        kernel,
        in_specs=[VMEM] * (3 + len(operands)),
        out_specs=[VMEM] * len(out_shape),
        out_shape=out_shape,
        scratch_shapes=[
            pltpu.VMEM((group, rows, width), dtype),
            pltpu.VMEM((group, rows, units), dtype),
            pltpu.VMEM((rows, units), jnp.float32),
        ],
        compiler_params=PARAMS,
        name="recur",
    )(w_input, w_hidden, bias, *operands)


def assemble(parts):
    group = len(parts)
    part_rows, width = parts[0].shape

    def kernel(*refs):
        out, sems = refs[-2:]
        half, place, lead = seat(group)
        copies = []
        for k in range(group):
            start = pl.multiple_of((lead ^ k) * part_rows, part_rows)
            target = out.at[0, pl.ds(start, part_rows)]
            copies.append(pltpu.make_async_copy(refs[k], target, sems.at[k]))
        for copy in copies:
            copy.start()
        for copy in copies:
            copy.wait()

    return pl.pallas_call(
        kernel,
        in_specs=[VMEM] * group,
        out_specs=ANY,
        out_shape=jax.ShapeDtypeStruct((1, group * part_rows, width), parts[0].dtype),
        scratch_shapes=[pltpu.SemaphoreType.DMA((group,))],
        compiler_params=PARAMS,
        name="assemble",
    )(*parts)


def send(array, target, lower_only=False):
    slab_count = lax.axis_size("slab")
    times = lax.axis_size("tm")
    pairs = []
    for time in range(times // 2 if lower_only else times):
        for slab in range(slab_count):
            to_time, to_slab = target(time, slab)
            pairs.append((time * slab_count + slab, to_time * slab_count + to_slab))
    return lax.ppermute(array, AXES, pairs)


def swap_slabs(arrays):
    got = list(arrays)
    for k in range(len(arrays) - 1, 0, -1):
        got[k] = send(arrays[k], lambda time, slab: (time, slab ^ k))
    return got


def swap_times(arrays):
    got = list(arrays)
    for k in range(len(arrays) - 1, 0, -1):
        got[k] = send(arrays[k], lambda time, slab: (time ^ k, slab))
    return got


def hand_over(last, group):
    flip = mirror(group)
    return send(last, lambda time, slab: (group + (time ^ flip), slab), lower_only=True)


def local(
    features, ref_lists, tile_rows, tile_sources, tile_counts, tile_values, w_input, w_hidden, bias
):
    row_count = features.shape[1]
    tile = tile_values.shape[2]
    slab_count = lax.axis_size("slab")
    layers = w_input.shape[0]
    group = lax.axis_size("tm") // 2
    half = lax.axis_index("tm") // group

    def mix(parts):
        listed = pick_tiles(parts, ref_lists, slab_count, row_count, tile, group, BOTH)
        arrived = swap_slabs(listed)
        mixed = convolve(
            arrived, tile_rows, tile_sources, tile_counts, tile_values, row_count, group, BOTH
        )
        return swap_times(mixed)

    def run(mixed, layer, mode, state=None, keep=()):
        return recur(mixed, layer, w_input, w_hidden, bias, mode, state, keep)

    upper_mixed = mix([features[0]])
    *hidden, last = run(upper_mixed, 0, LOWER)
    handed = hand_over(last, group)
    for layer in range(1, layers):

        def lower_layer(hidden, last):
            *hidden, last = run(mix(swap_times(hidden)), layer, BOTH)
            return hidden, last, half + 1

        def upper_layer(mixed, state):
            return mix(swap_times(run(mixed, layer - 1, BOTH, state)))

        hidden, last, turn = lax.cond(
            half == LOWER, lower_layer, lambda hidden, last: (hidden, last, half), hidden, last
        )
        following = hand_over(last, group)
        upper_mixed = lax.cond(
            half == turn, upper_layer, lambda mixed, state: mixed, upper_mixed, handed
        )
        handed = following
    return assemble(swap_times(run(upper_mixed, layers - 1, UPPER, handed, hidden)))


def solution(mesh):
    in_specs = (
        P("tm", "slab", None),
        P("tm", None, None),
        P("tm", "slab"),
        P("tm", "slab"),
        P("tm", "slab"),
        P("tm", "slab", None, None),
        P(),
        P(),
        P(),
    )
    out_specs = P("tm", "slab", None)
    return jax.shard_map(local, mesh=mesh, in_specs=in_specs, out_specs=out_specs, check_vma=False)
```

```python
import jax
import jax.numpy as jnp
from jax import lax
from jax.experimental import pallas as pl
from jax.experimental.pallas import tpu as pltpu
from jax.sharding import PartitionSpec as P


ANY = pl.BlockSpec(memory_space=pl.ANY)
SMEM = pl.BlockSpec(memory_space=pltpu.SMEM)
VMEM = pl.BlockSpec(memory_space=pltpu.VMEM)
PARAMS = pltpu.CompilerParams(vmem_limit_bytes=24 * 2**20)
UNROLL = 4
LANES = 128
CHUNKS = 2
AXES = ("tm", "slab")
LOWER, UPPER, BOTH = 0, 1, None


def seat(group):
    index = lax.axis_index("tm")
    half = index // group
    place = index % group
    return half, place, place ^ (half * mirror(group))


def mirror(group):
    return group - 2 if group > 2 else 0


def only(mode, half):
    def run(body):
        if mode is BOTH:
            body()
        else:
            pl.when(half == mode)(body)

    return run


def pick_tiles(parts, ref_table, slab_count, row_count, tile, group, column):
    part_count = len(parts)
    part_rows = parts[0].shape[0]
    listed = ref_table.shape[2] // slab_count

    def kernel(table, *refs):
        sources = refs[:part_count]
        outs = refs[part_count : part_count + slab_count]
        slab = lax.axis_index("slab")
        half, place, lead = seat(group)
        rows, first = sources[0], column * LANES
        if part_count > 1:
            rows, first = refs[-1], 0
            for k in range(part_count):
                start = pl.multiple_of((lead ^ k) * part_rows, part_rows)
                rows[pl.ds(start, part_rows), :] = sources[k][...]
        for k in reversed(range(slab_count)):
            for j in range(listed):
                index = table[0, slab ^ k, slab * listed + j]
                start = pl.multiple_of(index * tile, tile)
                outs[k][j * tile : (j + 1) * tile, :] = rows[
                    pl.ds(start, tile), first : first + LANES
                ]

    dtype = parts[0].dtype
    return pl.pallas_call(
        kernel,
        in_specs=[SMEM] + [VMEM] * part_count,
        out_specs=[VMEM] * slab_count,
        out_shape=[jax.ShapeDtypeStruct((listed * tile, LANES), dtype)] * slab_count,
        scratch_shapes=[pltpu.VMEM((row_count, LANES), dtype)] if part_count > 1 else [],
        compiler_params=PARAMS,
        name="pick_tiles",
    )(ref_table, *parts)


def convolve(arrived, tile_rows, tile_sources, tile_counts, tile_values, row_count, group):
    slab_count = len(arrived)
    piece, width = arrived[0].shape
    tile = tile_values.shape[2]
    group_rows = row_count // group

    def kernel(rows, sources, counts, values, *refs):
        pieces = refs[:slab_count]
        outs = refs[slab_count : slab_count + group]
        inputs, total = refs[slab_count + group :]
        slab = lax.axis_index("slab")
        half, place, lead = seat(group)

        for k in range(slab_count):
            start = pl.multiple_of((slab ^ k) * piece, piece)
            inputs[pl.ds(start, piece), :] = pieces[k][...]
        total[...] = jnp.zeros_like(total)
        count = counts[0, 0]

        def step(index, carry):
            products = []
            for lane in range(UNROLL):
                slot = index * UNROLL + lane
                start = pl.multiple_of(sources[0, slot] * tile, tile)
                product = jnp.dot(
                    values[0, slot],
                    inputs[pl.ds(start, tile), :],
                    preferred_element_type=jnp.float32,
                )
                products.append(jnp.where(slot < count, product, 0.0))
            for lane in range(UNROLL):
                target = pl.multiple_of(rows[0, index * UNROLL + lane] * tile, tile)
                total[pl.ds(target, tile), :] += products[lane]
            return carry

        lax.fori_loop(0, (count + UNROLL - 1) // UNROLL, step, 0)
        for k in range(group):
            start = pl.multiple_of((lead ^ k) * group_rows, group_rows)
            outs[k][...] = total[pl.ds(start, group_rows), :].astype(outs[k].dtype)

    dtype = arrived[0].dtype
    return pl.pallas_call(
        kernel,
        in_specs=[SMEM, SMEM, SMEM, VMEM] + [VMEM] * slab_count,
        out_specs=[VMEM] * group,
        out_shape=[jax.ShapeDtypeStruct((group_rows, width), dtype)] * group,
        scratch_shapes=[
            pltpu.VMEM((slab_count * piece, width), dtype),
            pltpu.VMEM((row_count, width), jnp.float32),
        ],
        compiler_params=PARAMS,
        name="convolve",
    )(tile_rows, tile_sources, tile_counts, tile_values, *arrived)


def sigmoid(value):
    return 0.5 * jnp.tanh(0.5 * value) + 0.5


def recur(mixed, layer, w_input, w_hidden, bias, mode, chunk, state=None, done=(), keep=()):
    columns, group = len(mixed), len(mixed[0])
    rows = mixed[0][0].shape[0]
    units = w_hidden.shape[1]
    size = rows // CHUNKS
    base = chunk * size
    final = chunk == CHUNKS - 1
    first = state is None
    blocks = [part for column in mixed for part in column]
    kept = [part for column in keep for part in column]
    operands = blocks + list(done) + kept + ([] if first else [state])
    outputs = units // LANES * group if final else 1

    def kernel(w_in, w_rec, gate_bias, *refs):
        earlier = refs[len(blocks) : len(blocks) + len(done)]
        start = refs[len(operands) - 1]
        outs = refs[len(operands) : len(operands) + outputs]
        inputs, states, memory = refs[-3:]
        half, place, lead = seat(group)

        if keep:

            @pl.when(half != mode)
            def _():
                for n in range(outputs):
                    outs[n][...] = refs[len(blocks) + len(done) + n][...]

        @only(mode, half)
        def _():
            for column in range(columns):
                lanes = slice(column * LANES, (column + 1) * LANES)
                for k in range(group):
                    source = refs[column * group + k]
                    inputs[place ^ k, :, lanes] = source[base : base + size, :]
            line = gate_bias[layer : layer + 1, :]

            def advance(gates, old, time):
                i, f, g, o = (gates[:, n * units : (n + 1) * units] for n in range(4))
                new = sigmoid(i) * jnp.tanh(g)
                if old is not None:
                    new = sigmoid(f) * old + new
                memory[...] = new
                states[time] = (sigmoid(o) * jnp.tanh(new)).astype(states.dtype)

            def project(time):
                return jnp.dot(inputs[time], w_in[layer], preferred_element_type=jnp.float32) + line

            def step(time, hidden):
                gates = project(time) + jnp.dot(
                    hidden, w_rec[layer], preferred_element_type=jnp.float32
                )
                advance(gates, memory[...], time)

            if first:
                advance(project(0), None, 0)
            else:
                memory[...] = start[1].astype(jnp.float32)
                step(0, start[0])

            def loop(time, carry):
                step(time, states[time - 1])
                return carry

            lax.fori_loop(1, group, loop, 0)
            if final:
                for column in range(units // LANES):
                    lanes = slice(column * LANES, (column + 1) * LANES)
                    for k in range(group):
                        out = outs[column * group + k]
                        out[base : base + size, :] = states[place ^ k, :, lanes]
                        for n in range(len(done)):
                            out[n * size : (n + 1) * size, :] = earlier[n][place ^ k, :, lanes]
            else:
                outs[0][...] = states[...]
            if first:
                last = refs[len(operands) + outputs]
                last[0] = states[group - 1]
                last[1] = memory[...].astype(last.dtype)

    dtype = mixed[0][0].dtype
    if final:
        out_shape = [jax.ShapeDtypeStruct((rows, LANES), dtype)] * outputs
    else:
        out_shape = [jax.ShapeDtypeStruct((group, size, units), dtype)]
    if first:
        out_shape.append(jax.ShapeDtypeStruct((2, size, units), dtype))
    results = pl.pallas_call(
        kernel,
        in_specs=[VMEM] * (3 + len(operands)),
        out_specs=[VMEM] * len(out_shape),
        out_shape=out_shape,
        scratch_shapes=[
            pltpu.VMEM((group, size, columns * LANES), dtype),
            pltpu.VMEM((group, size, units), dtype),
            pltpu.VMEM((size, units), jnp.float32),
        ],
        compiler_params=PARAMS,
        name="recur",
    )(w_input, w_hidden, bias, *operands)
    hidden = results[:outputs]
    if final:
        hidden = [hidden[n : n + group] for n in range(0, outputs, group)]
    else:
        hidden = hidden[0]
    return (hidden, results[-1]) if first else hidden


def assemble(parts):
    columns, group = len(parts), len(parts[0])
    part_rows = parts[0][0].shape[0]
    count = columns * group

    def kernel(*refs):
        out, sems = refs[-2:]
        half, place, lead = seat(group)
        copies = []
        for n in range(count):
            start = pl.multiple_of((lead ^ (n % group)) * part_rows, part_rows)
            lanes = pl.ds(n // group * LANES, LANES)
            target = out.at[0, pl.ds(start, part_rows), lanes]
            copies.append(pltpu.make_async_copy(refs[n], target, sems.at[n]))
        for copy in copies:
            copy.start()
        for copy in copies:
            copy.wait()

    return pl.pallas_call(
        kernel,
        in_specs=[VMEM] * count,
        out_specs=ANY,
        out_shape=jax.ShapeDtypeStruct(
            (1, group * part_rows, columns * LANES), parts[0][0].dtype
        ),
        scratch_shapes=[pltpu.SemaphoreType.DMA((count,))],
        compiler_params=PARAMS,
        name="assemble",
    )(*(part for column in parts for part in column))


def send(array, target, lower_only=False):
    slab_count = lax.axis_size("slab")
    times = lax.axis_size("tm")
    pairs = []
    for time in range(times // 2 if lower_only else times):
        for slab in range(slab_count):
            to_time, to_slab = target(time, slab)
            pairs.append((time * slab_count + slab, to_time * slab_count + to_slab))
    return lax.ppermute(array, AXES, pairs)


def swap_slabs(arrays):
    got = list(arrays)
    for k in range(len(arrays) - 1, 0, -1):
        got[k] = send(arrays[k], lambda time, slab: (time, slab ^ k))
    return got


def swap_times(arrays):
    got = list(arrays)
    for k in range(len(arrays) - 1, 0, -1):
        got[k] = send(arrays[k], lambda time, slab: (time ^ k, slab))
    return got


def hand_over(last, group):
    flip = mirror(group)
    return send(last, lambda time, slab: (group + (time ^ flip), slab), lower_only=True)


def local(
    features, ref_lists, tile_rows, tile_sources, tile_counts, tile_values, w_input, w_hidden, bias
):
    row_count = features.shape[1]
    tile = tile_values.shape[2]
    slab_count = lax.axis_size("slab")
    layers = w_input.shape[0]
    group = lax.axis_size("tm") // 2
    half = lax.axis_index("tm") // group

    def mix(parts, column=0):
        listed = pick_tiles(parts, ref_lists, slab_count, row_count, tile, group, column)
        arrived = swap_slabs(listed)
        return swap_times(
            convolve(
                arrived, tile_rows, tile_sources, tile_counts, tile_values, row_count, group
            )
        )

    def back_and_mix(hidden):
        return [mix(swap_times(column)) for column in hidden]

    def run(mixed, layer, mode, chunk, *rest):
        return recur(mixed, layer, w_input, w_hidden, bias, mode, chunk, *rest)

    def run_lower(mixed, layer, mode):
        done, lasts = [], []
        for chunk in range(CHUNKS):
            states, last = run(mixed, layer, mode, chunk, None, done)
            done.append(states)
            lasts.append(last)
        return states, lasts

    def run_upper(mixed, layer, states):
        done = []
        for chunk in range(CHUNKS - 1):
            done.append(run(mixed, layer, UPPER, chunk, states[chunk], done))
        return done

    features = features[0]
    upper_mixed = [mix([features], column) for column in range(features.shape[1] // LANES)]
    hidden, lasts = run_lower(upper_mixed, 0, LOWER)
    handed = [hand_over(last, group) for last in lasts]
    for layer in range(1, layers):

        def lower_layer(hidden, lasts):
            return *run_lower(back_and_mix(hidden), layer, BOTH), half + 1

        def upper_layer(mixed, done, state):
            return back_and_mix(run(mixed, layer - 1, BOTH, CHUNKS - 1, state, done))

        hidden, lasts, turn = lax.cond(
            half == LOWER, lower_layer, lambda hidden, lasts: (hidden, lasts, half), hidden, lasts
        )
        following = [hand_over(last, group) for last in lasts]
        done = run_upper(upper_mixed, layer - 1, handed)
        upper_mixed = lax.cond(
            half == turn,
            upper_layer,
            lambda mixed, done, state: mixed,
            upper_mixed,
            done,
            handed[-1],
        )
        handed = following
    done = run_upper(upper_mixed, layers - 1, handed)
    hidden = run(upper_mixed, layers - 1, UPPER, CHUNKS - 1, handed[-1], done, hidden)
    return assemble([swap_times(column) for column in hidden])


def solution(mesh):
    in_specs = (
        P("tm", "slab", None),
        P("tm", None, None),
        P("tm", "slab"),
        P("tm", "slab"),
        P("tm", "slab"),
        P("tm", "slab", None, None),
        P(),
        P(),
        P(),
    )
    out_specs = P("tm", "slab", None)
    return jax.shard_map(local, mesh=mesh, in_specs=in_specs, out_specs=out_specs, check_vma=False)
```

```python
import jax
import jax.numpy as jnp
from jax import lax
from jax.experimental import pallas as pl
from jax.experimental.pallas import tpu as pltpu
from jax.sharding import PartitionSpec as P


HBM = pl.BlockSpec(memory_space=pltpu.HBM)
VMEM = pl.BlockSpec(memory_space=pltpu.VMEM)
PARAMS = pltpu.CompilerParams(vmem_limit_bytes=16 * 2**20)
UNROLL = 4
LANES = 128
CHUNKS = 2
AXES = ("tm", "slab")
LOWER, UPPER, BOTH = 0, 1, None


def seat(group):
    index = lax.axis_index("tm")
    half = index // group
    place = index % group
    return half, place, place ^ (half * mirror(group))


def mirror(group):
    return group - 2 if group > 2 else 0


def only(mode, half):
    def run(body):
        if mode is BOTH:
            body()
        else:
            pl.when(half == mode)(body)

    return run


def pick_tiles(parts, ref_table, slab_count, row_count, tile, group, column):
    part_count = len(parts)
    part_rows = parts[0].shape[0]
    listed = ref_table.shape[2] // slab_count
    whole = part_count == 1

    def kernel(table_hbm, *refs):
        sources = refs[:part_count]
        outs = refs[part_count : part_count + slab_count]
        table, table_sem, rows, sems = refs[part_count + slab_count :]
        slab = lax.axis_index("slab")
        half, place, lead = seat(group)
        fetch = pltpu.make_async_copy(table_hbm, table, table_sem)
        fetch.start()
        if not whole:
            for k in range(part_count):
                start = pl.multiple_of((lead ^ k) * part_rows, part_rows)
                rows[pl.ds(start, part_rows), :] = sources[k][...]
        fetch.wait()
        copies = []
        for k in reversed(range(slab_count)):
            for j in range(listed):
                index = table[0, slab ^ k, slab * listed + j]
                start = pl.multiple_of(index * tile, tile)
                if whole:
                    source = sources[0].at[pl.ds(start, tile), pl.ds(column * LANES, LANES)]
                    target = outs[k].at[pl.ds(j * tile, tile)]
                    copies.append(pltpu.make_async_copy(source, target, sems.at[k, j]))
                else:
                    outs[k][j * tile : (j + 1) * tile, :] = rows[pl.ds(start, tile), :]
        for copy in copies:
            copy.start()
        for copy in copies:
            copy.wait()

    dtype = parts[0].dtype
    return pl.pallas_call(
        kernel,
        in_specs=[HBM] + [HBM if whole else VMEM] * part_count,
        out_specs=[VMEM] * slab_count,
        out_shape=[jax.ShapeDtypeStruct((listed * tile, LANES), dtype)] * slab_count,
        scratch_shapes=[
            pltpu.SMEM(ref_table.shape, ref_table.dtype),
            pltpu.SemaphoreType.DMA(()),
            pltpu.VMEM((tile if whole else row_count, LANES), dtype),
            pltpu.SemaphoreType.DMA((slab_count, listed)),
        ],
        compiler_params=PARAMS,
        name="pick_tiles",
    )(ref_table, *parts)


def convolve(arrived, tile_rows, tile_sources, tile_counts, tile_values, row_count, group):
    slab_count = len(arrived)
    piece, width = arrived[0].shape
    tile = tile_values.shape[2]
    group_rows = row_count // group

    tables = (tile_rows, tile_sources, tile_counts)

    def kernel(*refs):
        values = refs[3]
        pieces = refs[4 : 4 + slab_count]
        outs = refs[4 + slab_count : 4 + slab_count + group]
        rows, sources, counts, sems, inputs, total = refs[4 + slab_count + group :]
        slab = lax.axis_index("slab")
        half, place, lead = seat(group)
        fetches = [
            pltpu.make_async_copy(refs[n], local_ref, sems.at[n])
            for n, local_ref in enumerate((rows, sources, counts))
        ]
        for fetch in fetches:
            fetch.start()
        for k in range(slab_count):
            start = pl.multiple_of((slab ^ k) * piece, piece)
            inputs[pl.ds(start, piece), :] = pieces[k][...]
        total[...] = jnp.zeros_like(total)
        for fetch in fetches:
            fetch.wait()
        count = counts[0, 0]

        def step(index, carry):
            products = []
            for lane in range(UNROLL):
                slot = index * UNROLL + lane
                start = pl.multiple_of(sources[0, slot] * tile, tile)
                product = jnp.dot(
                    values[0, slot],
                    inputs[pl.ds(start, tile), :],
                    preferred_element_type=jnp.float32,
                )
                products.append(jnp.where(slot < count, product, 0.0))
            for lane in range(UNROLL):
                target = pl.multiple_of(rows[0, index * UNROLL + lane] * tile, tile)
                total[pl.ds(target, tile), :] += products[lane]
            return carry

        lax.fori_loop(0, (count + UNROLL - 1) // UNROLL, step, 0)
        for k in range(group):
            start = pl.multiple_of((lead ^ k) * group_rows, group_rows)
            outs[k][...] = total[pl.ds(start, group_rows), :].astype(outs[k].dtype)

    dtype = arrived[0].dtype
    return pl.pallas_call(
        kernel,
        in_specs=[HBM, HBM, HBM, VMEM] + [VMEM] * slab_count,
        out_specs=[VMEM] * group,
        out_shape=[jax.ShapeDtypeStruct((group_rows, width), dtype)] * group,
        scratch_shapes=[pltpu.SMEM(table.shape, table.dtype) for table in tables]
        + [
            pltpu.SemaphoreType.DMA((3,)),
            pltpu.VMEM((slab_count * piece, width), dtype),
            pltpu.VMEM((row_count, width), jnp.float32),
        ],
        compiler_params=PARAMS,
        name="convolve",
    )(*tables, tile_values, *arrived)


def sigmoid(value):
    return 0.5 * jnp.tanh(0.5 * value) + 0.5


def pack(mixed):
    columns, group = len(mixed), len(mixed[0])
    rows, lanes = mixed[0][0].shape
    blocks = [part for column in mixed for part in column]
    size = rows // CHUNKS

    def kernel(*refs):
        half, place, lead = seat(group)
        for n in range(len(blocks)):
            first = n // group * lanes
            for chunk, out in enumerate(refs[len(blocks) :]):
                source = refs[n][chunk * size : (chunk + 1) * size, :]
                out[place ^ (n % group), :, first : first + lanes] = source

    out_shape = jax.ShapeDtypeStruct((group, size, columns * lanes), blocks[0].dtype)
    return pl.pallas_call(
        kernel,
        in_specs=[VMEM] * len(blocks),
        out_specs=[VMEM] * CHUNKS,
        out_shape=[out_shape] * CHUNKS,
        compiler_params=PARAMS,
        name="pack",
    )(*blocks)


def spread_into(outs, chunks, place, group):
    lanes = outs[0].shape[1]
    for n, out in enumerate(outs):
        first = n // group * lanes
        base = 0
        for chunk in chunks:
            size = chunk.shape[1]
            out[base : base + size, :] = chunk[place ^ (n % group), :, first : first + lanes]
            base += size


def spread(chunks, lanes):
    group, size, units = chunks[0].shape
    count = units // lanes * group

    def kernel(*refs):
        half, place, lead = seat(group)
        spread_into(refs[len(chunks) :], refs[: len(chunks)], place, group)

    results = pl.pallas_call(
        kernel,
        in_specs=[VMEM] * len(chunks),
        out_specs=[VMEM] * count,
        out_shape=[jax.ShapeDtypeStruct((size * len(chunks), lanes), chunks[0].dtype)] * count,
        compiler_params=PARAMS,
        name="spread",
    )(*chunks)
    return [results[n : n + group] for n in range(0, count, group)]


def recur(mixed, layer, w_input, w_hidden, bias, mode, state=None, done=(), keep=(), lanes=0):
    group, size, width = mixed.shape
    units = w_hidden.shape[1]
    first = state is None
    operands = [mixed] + list(done) + list(keep) + ([] if first else [state])
    outputs = units // lanes * group if lanes else 1

    def kernel(w_in, w_rec, gate_bias, *refs):
        inputs = refs[0]
        earlier = refs[1 : 1 + len(done)]
        kept = refs[1 + len(done) : 1 + len(done) + len(keep)]
        start = refs[len(operands) - 1]
        outs = refs[len(operands) : len(operands) + outputs]
        memory = refs[-1]
        states = refs[-2] if lanes else outs[0]
        half, place, lead = seat(group)

        if keep:

            @pl.when(half != mode)
            def _():
                spread_into(outs, kept, place, group)

        @only(mode, half)
        def _():
            line = gate_bias[layer : layer + 1, :]

            def advance(gates, old, time):
                i, f, g, o = (gates[:, n * units : (n + 1) * units] for n in range(4))
                new = sigmoid(i) * jnp.tanh(g)
                if old is not None:
                    new = sigmoid(f) * old + new
                memory[...] = new
                states[time] = (sigmoid(o) * jnp.tanh(new)).astype(states.dtype)

            def project(time):
                return jnp.dot(inputs[time], w_in[layer], preferred_element_type=jnp.float32) + line

            def step(time, hidden):
                gates = project(time) + jnp.dot(
                    hidden, w_rec[layer], preferred_element_type=jnp.float32
                )
                advance(gates, memory[...], time)

            if first:
                advance(project(0), None, 0)
            else:
                memory[...] = start[1].astype(jnp.float32)
                step(0, start[0])

            def loop(time, carry):
                step(time, states[time - 1])
                return carry

            lax.fori_loop(1, group, loop, 0)
            if lanes:
                spread_into(outs, [*earlier, states], place, group)
            if first:
                last = refs[len(operands) + outputs]
                last[0] = states[group - 1]
                last[1] = memory[...].astype(last.dtype)

    dtype = mixed.dtype
    if lanes:
        out_shape = [jax.ShapeDtypeStruct((size * CHUNKS, lanes), dtype)] * outputs
    else:
        out_shape = [jax.ShapeDtypeStruct((group, size, units), dtype)]
    if first:
        out_shape.append(jax.ShapeDtypeStruct((2, size, units), dtype))
    scratch = [pltpu.VMEM((group, size, units), dtype)] if lanes else []
    results = pl.pallas_call(
        kernel,
        in_specs=[VMEM] * (3 + len(operands)),
        out_specs=[VMEM] * len(out_shape),
        out_shape=out_shape,
        scratch_shapes=scratch + [pltpu.VMEM((size, units), jnp.float32)],
        compiler_params=PARAMS,
        name="recur",
    )(w_input, w_hidden, bias, *operands)
    if lanes:
        return [results[n : n + group] for n in range(0, outputs, group)]
    return results if first else results[0]


def assemble(parts):
    columns, group = len(parts), len(parts[0])
    part_rows, part_lanes = parts[0][0].shape
    count = columns * group

    def kernel(*refs):
        out, sems = refs[-2:]
        half, place, lead = seat(group)
        copies = []
        for n in range(count):
            start = pl.multiple_of((lead ^ (n % group)) * part_rows, part_rows)
            lanes = pl.ds(n // group * part_lanes, part_lanes)
            target = out.at[0, pl.ds(start, part_rows), lanes]
            copies.append(pltpu.make_async_copy(refs[n], target, sems.at[n]))
        for copy in copies:
            copy.start()
        for copy in copies:
            copy.wait()

    return pl.pallas_call(
        kernel,
        in_specs=[VMEM] * count,
        out_specs=HBM,
        out_shape=jax.ShapeDtypeStruct(
            (1, group * part_rows, columns * part_lanes), parts[0][0].dtype
        ),
        scratch_shapes=[pltpu.SemaphoreType.DMA((count,))],
        compiler_params=PARAMS,
        name="assemble",
    )(*(part for column in parts for part in column))


def send(array, target, lower_only=False):
    slab_count = lax.axis_size("slab")
    times = lax.axis_size("tm")
    pairs = []
    for time in range(times // 2 if lower_only else times):
        for slab in range(slab_count):
            to_time, to_slab = target(time, slab)
            pairs.append((time * slab_count + slab, to_time * slab_count + to_slab))
    return lax.ppermute(array, AXES, pairs)


def swap_slabs(arrays):
    got = list(arrays)
    for k in range(len(arrays) - 1, 0, -1):
        got[k] = send(arrays[k], lambda time, slab: (time, slab ^ k))
    return got


def swap_times(arrays):
    got = list(arrays)
    for k in range(len(arrays) - 1, 0, -1):
        got[k] = send(arrays[k], lambda time, slab: (time ^ k, slab))
    return got


def hand_over(last, group):
    flip = mirror(group)
    return send(last, lambda time, slab: (group + (time ^ flip), slab), lower_only=True)


def local(
    features, ref_lists, tile_rows, tile_sources, tile_counts, tile_values, w_input, w_hidden, bias
):
    row_count = features.shape[1]
    tile = tile_values.shape[2]
    slab_count = lax.axis_size("slab")
    layers = w_input.shape[0]
    group = lax.axis_size("tm") // 2
    half = lax.axis_index("tm") // group

    def mix(parts, column=0):
        listed = pick_tiles(parts, ref_lists, slab_count, row_count, tile, group, column)
        arrived = swap_slabs(listed)
        return swap_times(
            convolve(
                arrived, tile_rows, tile_sources, tile_counts, tile_values, row_count, group
            )
        )

    def back_and_mix(hidden):
        return pack([mix(swap_times(column)) for column in hidden])

    def run(mixed, layer, mode, *rest):
        return recur(mixed, layer, w_input, w_hidden, bias, mode, *rest)

    def run_lower(mixed, layer, mode):
        chunks = [run(part, layer, mode) for part in mixed]
        return [states for states, last in chunks], [last for states, last in chunks]

    def run_upper(mixed, layer, states):
        return [run(part, layer, UPPER, state) for part, state in zip(mixed[:-1], states)]

    features = features[0]
    width = features.shape[1]
    upper_mixed = pack([mix([features], column) for column in range(width // LANES)])
    hidden, lasts = run_lower(upper_mixed, 0, LOWER)
    handed = [hand_over(last, group) for last in lasts]
    for layer in range(1, layers):

        def lower_layer(hidden, lasts):
            return *run_lower(back_and_mix(spread(hidden, LANES)), layer, BOTH), half + 1

        def upper_layer(mixed, done, state):
            return back_and_mix(run(mixed[-1], layer - 1, BOTH, state, done, (), LANES))

        hidden, lasts, turn = lax.cond(
            half == LOWER, lower_layer, lambda hidden, lasts: (hidden, lasts, half), hidden, lasts
        )
        following = [hand_over(last, group) for last in lasts]
        done = run_upper(upper_mixed, layer - 1, handed)
        upper_mixed = lax.cond(
            half == turn,
            upper_layer,
            lambda mixed, done, state: mixed,
            upper_mixed,
            done,
            handed[-1],
        )
        handed = following
    done = run_upper(upper_mixed, layers - 1, handed)
    units = w_hidden.shape[1]
    hidden = run(upper_mixed[-1], layers - 1, UPPER, handed[-1], done, hidden, units)
    return assemble([swap_times(column) for column in hidden])


def solution(mesh):
    in_specs = (
        P("tm", "slab", None),
        P("tm", None, None),
        P("tm", "slab"),
        P("tm", "slab"),
        P("tm", "slab"),
        P("tm", "slab", None, None),
        P(),
        P(),
        P(),
    )
    out_specs = P("tm", "slab", None)
    return jax.shard_map(local, mesh=mesh, in_specs=in_specs, out_specs=out_specs, check_vma=False)
```

```python
import jax
import jax.numpy as jnp
from jax import lax
from jax.experimental import pallas as pl
from jax.experimental.pallas import tpu as pltpu
from jax.sharding import PartitionSpec as P


HBM = pl.BlockSpec(memory_space=pltpu.HBM)
VMEM = pl.BlockSpec(memory_space=pltpu.VMEM)
PARAMS = pltpu.CompilerParams(vmem_limit_bytes=16 * 2**20)
UNROLL = 4
LANES = 128
CHUNKS = 2
AXES = ("tm", "slab")
LOWER, UPPER, BOTH = 0, 1, None


def seat(group):
    index = lax.axis_index("tm")
    half = index // group
    place = index % group
    return half, place, place ^ (half * mirror(group))


def mirror(group):
    return group - 2 if group > 2 else 0


def only(mode, half):
    def run(body):
        if mode is BOTH:
            body()
        else:
            pl.when(half == mode)(body)

    return run


def pick_tiles(parts, ref_table, slab_count, row_count, tile, group, column):
    part_count = len(parts)
    part_rows = parts[0].shape[0]
    listed = ref_table.shape[2] // slab_count
    whole = part_count == 1

    def kernel(table_hbm, *refs):
        sources = refs[:part_count]
        outs = refs[part_count : part_count + slab_count]
        table, table_sem, rows, sems = refs[part_count + slab_count :]
        slab = lax.axis_index("slab")
        _, _, lead = seat(group)
        fetch = pltpu.make_async_copy(table_hbm, table, table_sem)
        fetch.start()
        if not whole:
            for k in range(part_count):
                start = pl.multiple_of((lead ^ k) * part_rows, part_rows)
                rows[pl.ds(start, part_rows), :] = sources[k][...]
        fetch.wait()
        copies = []
        for k in reversed(range(slab_count)):
            for j in range(listed):
                index = table[0, slab ^ k, slab * listed + j]
                start = pl.multiple_of(index * tile, tile)
                if whole:
                    source = sources[0].at[pl.ds(start, tile), pl.ds(column * LANES, LANES)]
                    target = outs[k].at[pl.ds(j * tile, tile)]
                    copies.append(pltpu.make_async_copy(source, target, sems.at[k, j]))
                else:
                    outs[k][j * tile : (j + 1) * tile, :] = rows[pl.ds(start, tile), :]
        for copy in copies:
            copy.start()
        for copy in copies:
            copy.wait()

    dtype = parts[0].dtype
    return pl.pallas_call(
        kernel,
        in_specs=[HBM] + [HBM if whole else VMEM] * part_count,
        out_specs=[VMEM] * slab_count,
        out_shape=[jax.ShapeDtypeStruct((listed * tile, LANES), dtype)] * slab_count,
        scratch_shapes=[
            pltpu.SMEM(ref_table.shape, ref_table.dtype),
            pltpu.SemaphoreType.DMA(()),
            pltpu.VMEM((tile if whole else row_count, LANES), dtype),
            pltpu.SemaphoreType.DMA((slab_count, listed)),
        ],
        compiler_params=PARAMS,
        name="pick_tiles",
    )(ref_table, *parts)


def convolve(arrived, tile_rows, tile_sources, tile_counts, tile_values, row_count, group):
    slab_count = len(arrived)
    piece, width = arrived[0].shape
    tile = tile_values.shape[2]
    group_rows = row_count // group

    tables = (tile_rows, tile_sources, tile_counts)

    def kernel(*refs):
        values = refs[3]
        pieces = refs[4 : 4 + slab_count]
        outs = refs[4 + slab_count : 4 + slab_count + group]
        rows, sources, counts, sems, inputs, total = refs[4 + slab_count + group :]
        slab = lax.axis_index("slab")
        _, _, lead = seat(group)
        fetches = [
            pltpu.make_async_copy(refs[n], local_ref, sems.at[n])
            for n, local_ref in enumerate((rows, sources, counts))
        ]
        for fetch in fetches:
            fetch.start()
        for k in range(slab_count):
            start = pl.multiple_of((slab ^ k) * piece, piece)
            inputs[pl.ds(start, piece), :] = pieces[k][...]
        total[...] = jnp.zeros_like(total)
        for fetch in fetches:
            fetch.wait()
        count = counts[0, 0]

        def step(index, carry):
            products = []
            for lane in range(UNROLL):
                slot = index * UNROLL + lane
                start = pl.multiple_of(sources[0, slot] * tile, tile)
                product = jnp.dot(
                    values[0, slot],
                    inputs[pl.ds(start, tile), :],
                    preferred_element_type=jnp.float32,
                )
                products.append(jnp.where(slot < count, product, 0.0))
            for lane in range(UNROLL):
                target = pl.multiple_of(rows[0, index * UNROLL + lane] * tile, tile)
                total[pl.ds(target, tile), :] += products[lane]
            return carry

        lax.fori_loop(0, (count + UNROLL - 1) // UNROLL, step, 0)
        for k in range(group):
            start = pl.multiple_of((lead ^ k) * group_rows, group_rows)
            outs[k][...] = total[pl.ds(start, group_rows), :].astype(outs[k].dtype)

    dtype = arrived[0].dtype
    return pl.pallas_call(
        kernel,
        in_specs=[HBM, HBM, HBM, VMEM] + [VMEM] * slab_count,
        out_specs=[VMEM] * group,
        out_shape=[jax.ShapeDtypeStruct((group_rows, width), dtype)] * group,
        scratch_shapes=[pltpu.SMEM(table.shape, table.dtype) for table in tables]
        + [
            pltpu.SemaphoreType.DMA((3,)),
            pltpu.VMEM((slab_count * piece, width), dtype),
            pltpu.VMEM((row_count, width), jnp.float32),
        ],
        compiler_params=PARAMS,
        name="convolve",
    )(*tables, tile_values, *arrived)


def sigmoid(value):
    return 0.5 * jnp.tanh(0.5 * value) + 0.5


def pack(mixed):
    columns, group = len(mixed), len(mixed[0])
    rows, lanes = mixed[0][0].shape
    blocks = [part for column in mixed for part in column]
    size = rows // CHUNKS

    def kernel(*refs):
        _, place, _ = seat(group)
        for n in range(len(blocks)):
            first = n // group * lanes
            for chunk, out in enumerate(refs[len(blocks) :]):
                source = refs[n][chunk * size : (chunk + 1) * size, :]
                out[place ^ (n % group), :, first : first + lanes] = source

    out_shape = jax.ShapeDtypeStruct((group, size, columns * lanes), blocks[0].dtype)
    return list(pl.pallas_call(
        kernel,
        in_specs=[VMEM] * len(blocks),
        out_specs=[VMEM] * CHUNKS,
        out_shape=[out_shape] * CHUNKS,
        compiler_params=PARAMS,
        name="pack",
    )(*blocks))


def spread_into(outs, chunks, place, group):
    lanes = outs[0].shape[1]
    for n, out in enumerate(outs):
        first = n // group * lanes
        base = 0
        for chunk in chunks:
            size = chunk.shape[1]
            out[base : base + size, :] = chunk[place ^ (n % group), :, first : first + lanes]
            base += size


def spread(chunks, lanes):
    group, size, units = chunks[0].shape
    count = units // lanes * group

    def kernel(*refs):
        _, place, _ = seat(group)
        spread_into(refs[len(chunks) :], refs[: len(chunks)], place, group)

    results = pl.pallas_call(
        kernel,
        in_specs=[VMEM] * len(chunks),
        out_specs=[VMEM] * count,
        out_shape=[jax.ShapeDtypeStruct((size * len(chunks), lanes), chunks[0].dtype)] * count,
        compiler_params=PARAMS,
        name="spread",
    )(*chunks)
    return [results[n : n + group] for n in range(0, count, group)]


def recur(mixed, layer, w_input, w_hidden, bias, mode, state=None, done=(), keep=(), lanes=0):
    group, size, _ = mixed.shape
    units = w_hidden.shape[1]
    first = state is None
    operands = [mixed] + list(done) + list(keep) + ([] if first else [state])
    outputs = units // lanes * group if lanes else 1

    def kernel(w_in, w_rec, gate_bias, *refs):
        inputs = refs[0]
        earlier = refs[1 : 1 + len(done)]
        kept = refs[1 + len(done) : 1 + len(done) + len(keep)]
        start = refs[len(operands) - 1]
        outs = refs[len(operands) : len(operands) + outputs]
        memory = refs[-1]
        states = refs[-2] if lanes else outs[0]
        half, place, _ = seat(group)

        if keep:

            @pl.when(half != mode)
            def _():
                spread_into(outs, kept, place, group)

        @only(mode, half)
        def _():
            line = gate_bias[layer : layer + 1, :]

            def advance(gates, old, time):
                i, f, g, o = (gates[:, n * units : (n + 1) * units] for n in range(4))
                new = sigmoid(i) * jnp.tanh(g)
                if old is not None:
                    new = sigmoid(f) * old + new
                memory[...] = new
                states[time] = (sigmoid(o) * jnp.tanh(new)).astype(states.dtype)

            def project(time):
                return jnp.dot(inputs[time], w_in[layer], preferred_element_type=jnp.float32) + line

            def step(time, hidden):
                gates = project(time) + jnp.dot(
                    hidden, w_rec[layer], preferred_element_type=jnp.float32
                )
                advance(gates, memory[...], time)

            if first:
                advance(project(0), None, 0)
            else:
                memory[...] = start[1].astype(jnp.float32)
                step(0, start[0])

            def loop(time, carry):
                step(time, states[time - 1])
                return carry

            lax.fori_loop(1, group, loop, 0)
            if lanes:
                spread_into(outs, [*earlier, states], place, group)
            if first:
                last = refs[len(operands) + outputs]
                last[0] = states[group - 1]
                last[1] = memory[...].astype(last.dtype)

    dtype = mixed.dtype
    if lanes:
        out_shape = [jax.ShapeDtypeStruct((size * CHUNKS, lanes), dtype)] * outputs
    else:
        out_shape = [jax.ShapeDtypeStruct((group, size, units), dtype)]
    if first:
        out_shape.append(jax.ShapeDtypeStruct((2, size, units), dtype))
    scratch = [pltpu.VMEM((group, size, units), dtype)] if lanes else []
    results = pl.pallas_call(
        kernel,
        in_specs=[VMEM] * (3 + len(operands)),
        out_specs=[VMEM] * len(out_shape),
        out_shape=out_shape,
        scratch_shapes=scratch + [pltpu.VMEM((size, units), jnp.float32)],
        compiler_params=PARAMS,
        name="recur",
    )(w_input, w_hidden, bias, *operands)
    if lanes:
        return [results[n : n + group] for n in range(0, outputs, group)]
    return results if first else results[0]


def assemble(parts):
    columns, group = len(parts), len(parts[0])
    part_rows, part_lanes = parts[0][0].shape
    count = columns * group

    def kernel(*refs):
        out, sems = refs[-2:]
        _, _, lead = seat(group)
        copies = []
        for n in range(count):
            start = pl.multiple_of((lead ^ (n % group)) * part_rows, part_rows)
            lanes = pl.ds(n // group * part_lanes, part_lanes)
            target = out.at[0, pl.ds(start, part_rows), lanes]
            copies.append(pltpu.make_async_copy(refs[n], target, sems.at[n]))
        for copy in copies:
            copy.start()
        for copy in copies:
            copy.wait()

    return pl.pallas_call(
        kernel,
        in_specs=[VMEM] * count,
        out_specs=HBM,
        out_shape=jax.ShapeDtypeStruct(
            (1, group * part_rows, columns * part_lanes), parts[0][0].dtype
        ),
        scratch_shapes=[pltpu.SemaphoreType.DMA((count,))],
        compiler_params=PARAMS,
        name="assemble",
    )(*(part for column in parts for part in column))


def send(array, target, lower_only=False):
    slab_count = lax.axis_size("slab")
    times = lax.axis_size("tm")
    pairs = []
    for time in range(times // 2 if lower_only else times):
        for slab in range(slab_count):
            to_time, to_slab = target(time, slab)
            pairs.append((time * slab_count + slab, to_time * slab_count + to_slab))
    return lax.ppermute(array, AXES, pairs)


def swap_slabs(arrays):
    got = list(arrays)
    for k in range(len(arrays) - 1, 0, -1):
        got[k] = send(arrays[k], lambda time, slab: (time, slab ^ k))
    return got


def swap_times(arrays):
    got = list(arrays)
    for k in range(len(arrays) - 1, 0, -1):
        got[k] = send(arrays[k], lambda time, slab: (time ^ k, slab))
    return got


def hand_over(last, group):
    flip = mirror(group)
    return send(last, lambda time, slab: (group + (time ^ flip), slab), lower_only=True)


def local(
    features, ref_lists, tile_rows, tile_sources, tile_counts, tile_values, w_input, w_hidden, bias
):
    row_count = features.shape[1]
    tile = tile_values.shape[2]
    slab_count = lax.axis_size("slab")
    layers = w_input.shape[0]
    group = lax.axis_size("tm") // 2
    half = lax.axis_index("tm") // group

    def mix(parts, column=0):
        listed = pick_tiles(parts, ref_lists, slab_count, row_count, tile, group, column)
        arrived = swap_slabs(listed)
        return swap_times(
            convolve(
                arrived, tile_rows, tile_sources, tile_counts, tile_values, row_count, group
            )
        )

    def back_and_mix(hidden):
        return pack([mix(swap_times(column)) for column in hidden])

    def run(mixed, layer, mode, *rest):
        return recur(mixed, layer, w_input, w_hidden, bias, mode, *rest)

    def run_lower(mixed, layer):
        chunks, handed = [], []
        for part in mixed:
            states, last = run(part, layer, LOWER)
            handed.append(hand_over(last, group))
            chunks.append(states)
        return chunks, handed

    def run_upper(mixed, layer, states):
        return [run(part, layer, UPPER, state) for part, state in zip(mixed[:-1], states)]

    features = features[0]
    width = features.shape[1]
    upper_mixed = pack([mix([features], column) for column in range(width // LANES)])
    hidden, handed = run_lower(upper_mixed, 0)
    for layer in range(1, layers):

        def lower_layer(hidden):
            return back_and_mix(spread(hidden, LANES)), half + 1

        def upper_layer(mixed, done, state):
            return back_and_mix(run(mixed[-1], layer - 1, BOTH, state, done, (), LANES))

        lower_mixed, turn = lax.cond(
            half == LOWER, lower_layer, lambda hidden: (hidden, half), hidden
        )
        hidden, following = run_lower(lower_mixed, layer)
        done = run_upper(upper_mixed, layer - 1, handed)
        upper_mixed = lax.cond(
            half == turn,
            upper_layer,
            lambda mixed, done, state: mixed,
            upper_mixed,
            done,
            handed[-1],
        )
        handed = following
    done = run_upper(upper_mixed, layers - 1, handed)
    units = w_hidden.shape[1]
    hidden = run(upper_mixed[-1], layers - 1, UPPER, handed[-1], done, hidden, units)
    return assemble([swap_times(column) for column in hidden])


def solution(mesh):
    in_specs = (
        P("tm", "slab", None),
        P("tm", None, None),
        P("tm", "slab"),
        P("tm", "slab"),
        P("tm", "slab"),
        P("tm", "slab", None, None),
        P(),
        P(),
        P(),
    )
    out_specs = P("tm", "slab", None)
    return jax.shard_map(local, mesh=mesh, in_specs=in_specs, out_specs=out_specs, check_vma=False)
```

```python
import jax
import jax.numpy as jnp
from jax import lax
from jax.experimental import pallas as pl
from jax.experimental.pallas import tpu as pltpu
from jax.sharding import PartitionSpec as P


HBM = pl.BlockSpec(memory_space=pltpu.HBM)
VMEM = pl.BlockSpec(memory_space=pltpu.VMEM)
PARAMS = pltpu.CompilerParams(vmem_limit_bytes=16 * 2**20)
UNROLL = 32
LANES = 128
CHUNKS = 2
AXES = ("tm", "slab")
LOWER, UPPER, BOTH = 0, 1, None


def seat(group):
    index = lax.axis_index("tm")
    half = index // group
    place = index % group
    return half, place, place ^ (half * mirror(group))


def mirror(group):
    return group - 2 if group > 2 else 0


def only(mode, half):
    def run(body):
        if mode is BOTH:
            body()
        else:
            pl.when(half == mode)(body)

    return run


def pick_tiles(parts, ref_table, slab_count, row_count, tile, group, column, carried=()):
    part_count = len(parts)
    part_rows = parts[0].shape[0]
    listed = ref_table.shape[2] // slab_count
    whole = part_count == 1

    def kernel(table_hbm, *refs):
        sources = refs[:part_count]
        first_out = part_count + len(carried)
        outs = refs[first_out : first_out + slab_count]
        table, table_sem, rows, sems = refs[-4:]
        slab = lax.axis_index("slab")
        _, _, lead = seat(group)
        fetch = pltpu.make_async_copy(table_hbm, table, table_sem)
        fetch.start()
        if not whole:
            for k in range(part_count):
                start = pl.multiple_of((lead ^ k) * part_rows, part_rows)
                rows[pl.ds(start, part_rows), :] = sources[k][...]
        fetch.wait()
        copies = []
        for k in reversed(range(slab_count)):
            for j in range(listed):
                index = table[0, slab ^ k, slab * listed + j]
                start = pl.multiple_of(index * tile, tile)
                if whole:
                    source = sources[0].at[pl.ds(start, tile), pl.ds(column * LANES, LANES)]
                    target = outs[k].at[pl.ds(j * tile, tile)]
                    copies.append(pltpu.make_async_copy(source, target, sems.at[k, j]))
                else:
                    outs[k][j * tile : (j + 1) * tile, :] = rows[pl.ds(start, tile), :]
        for copy in copies:
            copy.start()
        for n in range(len(carried)):
            refs[first_out + slab_count + n][...] = refs[part_count + n][...]
        for copy in copies:
            copy.wait()

    dtype = parts[0].dtype
    results = pl.pallas_call(
        kernel,
        in_specs=[HBM] + [HBM if whole else VMEM] * part_count + [VMEM] * len(carried),
        out_specs=[VMEM] * (slab_count + len(carried)),
        out_shape=[jax.ShapeDtypeStruct((listed * tile, LANES), dtype)] * slab_count
        + [jax.ShapeDtypeStruct(array.shape, array.dtype) for array in carried],
        scratch_shapes=[
            pltpu.SMEM(ref_table.shape, ref_table.dtype),
            pltpu.SemaphoreType.DMA(()),
            pltpu.VMEM((tile if whole else row_count, LANES), dtype),
            pltpu.SemaphoreType.DMA((slab_count, listed)),
        ],
        compiler_params=PARAMS,
        name="pick_tiles",
    )(ref_table, *parts, *carried)
    return results[:slab_count], results[slab_count:]


def convolve(arrived, tile_rows, tile_sources, tile_counts, tile_values, row_count, group):
    slab_count = len(arrived)
    piece, width = arrived[0].shape
    tile = tile_values.shape[2]
    group_rows = row_count // group

    tables = (tile_rows, tile_sources, tile_counts)
    unroll = min(UNROLL, tile_values.shape[1])

    def kernel(*refs):
        values = refs[3]
        pieces = refs[4 : 4 + slab_count]
        outs = refs[4 + slab_count : 4 + slab_count + group]
        rows, sources, counts, sems, inputs, total = refs[4 + slab_count + group :]
        slab = lax.axis_index("slab")
        _, _, lead = seat(group)
        fetches = [
            pltpu.make_async_copy(refs[n], local_ref, sems.at[n])
            for n, local_ref in enumerate((rows, sources, counts))
        ]
        for fetch in fetches:
            fetch.start()
        for k in range(slab_count):
            start = pl.multiple_of((slab ^ k) * piece, piece)
            inputs[pl.ds(start, piece), :] = pieces[k][...]
        total[...] = jnp.zeros_like(total)
        for fetch in fetches:
            fetch.wait()
        count = counts[0, 0]

        def step(index, carry):
            products = []
            for lane in range(unroll):
                slot = index * unroll + lane
                start = pl.multiple_of(sources[0, slot] * tile, tile)
                product = jnp.dot(
                    values[0, slot],
                    inputs[pl.ds(start, tile), :],
                    preferred_element_type=jnp.float32,
                )
                products.append(jnp.where(slot < count, product, 0.0))
            for lane in range(unroll):
                target = pl.multiple_of(rows[0, index * unroll + lane] * tile, tile)
                total[pl.ds(target, tile), :] += products[lane]
            return carry

        lax.fori_loop(0, (count + unroll - 1) // unroll, step, 0)
        for k in range(group):
            start = pl.multiple_of((lead ^ k) * group_rows, group_rows)
            outs[k][...] = total[pl.ds(start, group_rows), :].astype(outs[k].dtype)

    dtype = arrived[0].dtype
    return pl.pallas_call(
        kernel,
        in_specs=[HBM, HBM, HBM, VMEM] + [VMEM] * slab_count,
        out_specs=[VMEM] * group,
        out_shape=[jax.ShapeDtypeStruct((group_rows, width), dtype)] * group,
        scratch_shapes=[pltpu.SMEM(table.shape, table.dtype) for table in tables]
        + [
            pltpu.SemaphoreType.DMA((3,)),
            pltpu.VMEM((slab_count * piece, width), dtype),
            pltpu.VMEM((row_count, width), jnp.float32),
        ],
        compiler_params=PARAMS,
        name="convolve",
    )(*tables, tile_values, *arrived)


def sigmoid(value):
    return 0.5 * jnp.tanh(0.5 * value) + 0.5


def pack(mixed):
    columns, group = len(mixed), len(mixed[0])
    rows, lanes = mixed[0][0].shape
    blocks = [part for column in mixed for part in column]
    size = rows // CHUNKS

    def kernel(*refs):
        _, place, _ = seat(group)
        for n in range(len(blocks)):
            first = n // group * lanes
            for chunk, out in enumerate(refs[len(blocks) :]):
                source = refs[n][chunk * size : (chunk + 1) * size, :]
                out[place ^ (n % group), :, first : first + lanes] = source

    out_shape = jax.ShapeDtypeStruct((group, size, columns * lanes), blocks[0].dtype)
    return list(pl.pallas_call(
        kernel,
        in_specs=[VMEM] * len(blocks),
        out_specs=[VMEM] * CHUNKS,
        out_shape=[out_shape] * CHUNKS,
        compiler_params=PARAMS,
        name="pack",
    )(*blocks))


def spread_into(outs, chunks, place, group):
    lanes = outs[0].shape[1]
    for n, out in enumerate(outs):
        first = n // group * lanes
        base = 0
        for chunk in chunks:
            size = chunk.shape[1]
            out[base : base + size, :] = chunk[place ^ (n % group), :, first : first + lanes]
            base += size


def spread(chunks, lanes):
    group, size, units = chunks[0].shape
    count = units // lanes * group

    def kernel(*refs):
        _, place, _ = seat(group)
        spread_into(refs[len(chunks) :], refs[: len(chunks)], place, group)

    results = pl.pallas_call(
        kernel,
        in_specs=[VMEM] * len(chunks),
        out_specs=[VMEM] * count,
        out_shape=[jax.ShapeDtypeStruct((size * len(chunks), lanes), chunks[0].dtype)] * count,
        compiler_params=PARAMS,
        name="spread",
    )(*chunks)
    return [results[n : n + group] for n in range(0, count, group)]


def recur(mixed, layer, w_input, w_hidden, bias, mode, state=None, done=(), keep=(), lanes=0):
    group, size, _ = mixed.shape
    units = w_hidden.shape[1]
    first = state is None
    operands = [mixed] + list(done) + list(keep) + ([] if first else [state])
    outputs = units // lanes * group if lanes else 1

    def kernel(w_in, w_rec, gate_bias, *refs):
        inputs = refs[0]
        earlier = refs[1 : 1 + len(done)]
        kept = refs[1 + len(done) : 1 + len(done) + len(keep)]
        start = refs[len(operands) - 1]
        outs = refs[len(operands) : len(operands) + outputs]
        memory = refs[-1]
        states = refs[-2] if lanes else outs[0]
        half, place, _ = seat(group)

        if keep:

            @pl.when(half != mode)
            def _():
                spread_into(outs, kept, place, group)

        @only(mode, half)
        def _():
            line = gate_bias[layer : layer + 1, :]

            def advance(gates, old, time):
                i, f, g, o = (gates[:, n * units : (n + 1) * units] for n in range(4))
                new = sigmoid(i) * jnp.tanh(g)
                if old is not None:
                    new = sigmoid(f) * old + new
                memory[...] = new
                states[time] = (sigmoid(o) * jnp.tanh(new)).astype(states.dtype)

            def project(time):
                return jnp.dot(inputs[time], w_in[layer], preferred_element_type=jnp.float32) + line

            def step(time, hidden):
                gates = project(time) + jnp.dot(
                    hidden, w_rec[layer], preferred_element_type=jnp.float32
                )
                advance(gates, memory[...], time)

            if first:
                advance(project(0), None, 0)
            else:
                memory[...] = start[1].astype(jnp.float32)
                step(0, start[0])

            def loop(time, carry):
                step(time, states[time - 1])
                return carry

            lax.fori_loop(1, group, loop, 0, unroll=True)
            if lanes:
                spread_into(outs, [*earlier, states], place, group)
            if first:
                last = refs[len(operands) + outputs]
                last[0] = states[group - 1]
                last[1] = memory[...].astype(last.dtype)

    dtype = mixed.dtype
    if lanes:
        out_shape = [jax.ShapeDtypeStruct((size * (1 + len(done)), lanes), dtype)] * outputs
    else:
        out_shape = [jax.ShapeDtypeStruct((group, size, units), dtype)]
    if first:
        out_shape.append(jax.ShapeDtypeStruct((2, size, units), dtype))
    scratch = [pltpu.VMEM((group, size, units), dtype)] if lanes else []
    results = pl.pallas_call(
        kernel,
        in_specs=[VMEM] * (3 + len(operands)),
        out_specs=[VMEM] * len(out_shape),
        out_shape=out_shape,
        scratch_shapes=scratch + [pltpu.VMEM((size, units), jnp.float32)],
        compiler_params=PARAMS,
        name="recur",
    )(w_input, w_hidden, bias, *operands)
    if lanes:
        return [results[n : n + group] for n in range(0, outputs, group)]
    return results if first else results[0]


def assemble(parts):
    group = len(parts[0])
    size, width = parts[0][0].shape
    part_rows = size * len(parts)
    count = len(parts) * group

    def kernel(*refs):
        out, sems = refs[-2:]
        _, _, lead = seat(group)
        copies = []
        for n in range(count):
            start = (lead ^ (n % group)) * part_rows + n // group * size
            target = out.at[0, pl.ds(pl.multiple_of(start, size), size)]
            copies.append(pltpu.make_async_copy(refs[n], target, sems.at[n]))
        for copy in copies:
            copy.start()
        for copy in copies:
            copy.wait()

    return pl.pallas_call(
        kernel,
        in_specs=[VMEM] * count,
        out_specs=HBM,
        out_shape=jax.ShapeDtypeStruct((1, group * part_rows, width), parts[0][0].dtype),
        scratch_shapes=[pltpu.SemaphoreType.DMA((count,))],
        compiler_params=PARAMS,
        name="assemble",
    )(*(part for chunk in parts for part in chunk))


def send(array, target, lower_only=False):
    slab_count = lax.axis_size("slab")
    times = lax.axis_size("tm")
    pairs = []
    for time in range(times // 2 if lower_only else times):
        for slab in range(slab_count):
            to_time, to_slab = target(time, slab)
            pairs.append((time * slab_count + slab, to_time * slab_count + to_slab))
    return lax.ppermute(array, AXES, pairs)


def swap_slabs(arrays):
    got = list(arrays)
    for k in range(len(arrays) - 1, 0, -1):
        got[k] = send(arrays[k], lambda time, slab: (time, slab ^ k))
    return got


def swap_times(arrays):
    got = list(arrays)
    for k in range(len(arrays) - 1, 0, -1):
        got[k] = send(arrays[k], lambda time, slab: (time ^ k, slab))
    return got


def hand_over(last, group):
    flip = mirror(group)
    return send(last, lambda time, slab: (group + (time ^ flip), slab), lower_only=True)


def local(
    features, ref_lists, tile_rows, tile_sources, tile_counts, tile_values, w_input, w_hidden, bias
):
    row_count = features.shape[1]
    tile = tile_values.shape[2]
    slab_count = lax.axis_size("slab")
    layers = w_input.shape[0]
    group = lax.axis_size("tm") // 2
    half = lax.axis_index("tm") // group

    def pick(parts, table, column=0, carried=()):
        return pick_tiles(parts, table, slab_count, row_count, tile, group, column, carried)

    def mix(listed):
        arrived = swap_slabs(listed)
        return swap_times(
            convolve(
                arrived, tile_rows, tile_sources, tile_counts, tile_values, row_count, group
            )
        )

    def back_and_mix(hidden):
        return pack([mix(pick(swap_times(column), table)[0]) for column in hidden])

    def run(mixed, layer, mode, *rest):
        return recur(mixed, layer, w_input, w_hidden, gate_bias, mode, *rest)

    def run_lower(mixed, layer):
        chunks, handed = [], []
        for part in mixed:
            states, last = run(part, layer, LOWER)
            handed.append(hand_over(last, group))
            chunks.append(states)
        return chunks, handed

    def run_upper(mixed, layer, states):
        return [run(part, layer, UPPER, state) for part, state in zip(mixed[:-1], states)]

    features = features[0]
    columns = features.shape[1] // LANES
    listed = [pick([features], ref_lists, column)[0] for column in range(columns - 1)]
    last, (table, gate_bias) = pick([features], ref_lists, columns - 1, (ref_lists, bias))
    upper_mixed = pack([mix(column) for column in [*listed, last]])
    hidden, handed = run_lower(upper_mixed, 0)
    for layer in range(1, layers):

        def lower_layer(hidden):
            return back_and_mix(spread(hidden, LANES)), half + 1

        def upper_layer(mixed, done, state):
            return back_and_mix(run(mixed[-1], layer - 1, BOTH, state, done, (), LANES))

        lower_mixed, turn = lax.cond(
            half == LOWER, lower_layer, lambda hidden: (hidden, half), hidden
        )
        hidden, following = run_lower(lower_mixed, layer)
        done = run_upper(upper_mixed, layer - 1, handed)
        upper_mixed = lax.cond(
            half == turn,
            upper_layer,
            lambda mixed, done, state: mixed,
            upper_mixed,
            done,
            handed[-1],
        )
        handed = following
    units = w_hidden.shape[1]
    parts = []
    for number, (part, state) in enumerate(zip(upper_mixed, handed)):
        (states,) = run(part, layers - 1, UPPER, state, (), hidden[number : number + 1], units)
        parts.append(swap_times(states))
    return assemble(parts)


def solution(mesh):
    in_specs = (
        P("tm", "slab", None),
        P("tm", None, None),
        P("tm", "slab"),
        P("tm", "slab"),
        P("tm", "slab"),
        P("tm", "slab", None, None),
        P(),
        P(),
        P(),
    )
    out_specs = P("tm", "slab", None)
    return jax.shard_map(local, mesh=mesh, in_specs=in_specs, out_specs=out_specs, check_vma=False)
```

```python
import jax
import jax.numpy as jnp
from jax import lax
from jax.experimental import pallas as pl
from jax.experimental.pallas import tpu as pltpu
from jax.sharding import PartitionSpec as P


HBM = pl.BlockSpec(memory_space=pltpu.HBM)
VMEM = pl.BlockSpec(memory_space=pltpu.VMEM)
PARAMS = pltpu.CompilerParams(vmem_limit_bytes=16 * 2**20)
BATCH = 8
LANES = 128
CHUNKS = 2
AXES = ("tm", "slab")
LOWER, UPPER, BOTH = 0, 1, None


def seat(group):
    index = lax.axis_index("tm")
    half = index // group
    place = index % group
    return half, place, place ^ (half * mirror(group))


def mirror(group):
    return group - 2 if group > 2 else 0


def only(mode, half):
    def run(body):
        if mode is BOTH:
            body()
        else:
            pl.when(half == mode)(body)

    return run


def pick_tiles(parts, ref_table, slab_count, row_count, tile, group, column, carried=()):
    part_count = len(parts)
    part_rows = parts[0].shape[0]
    listed = ref_table.shape[2] // slab_count
    whole = part_count == 1

    def kernel(table_hbm, *refs):
        sources = refs[:part_count]
        first_out = part_count + len(carried)
        outs = refs[first_out : first_out + slab_count]
        table, table_sem, rows, sems = refs[-4:]
        slab = lax.axis_index("slab")
        _, _, lead = seat(group)
        fetch = pltpu.make_async_copy(table_hbm, table, table_sem)
        fetch.start()
        if not whole:
            for k in range(part_count):
                start = pl.multiple_of((lead ^ k) * part_rows, part_rows)
                rows[pl.ds(start, part_rows), :] = sources[k][...]
        fetch.wait()
        copies = []
        for k in reversed(range(slab_count)):
            for j in range(listed):
                index = table[0, slab ^ k, slab * listed + j]
                start = pl.multiple_of(index * tile, tile)
                if whole:
                    source = sources[0].at[pl.ds(start, tile), pl.ds(column * LANES, LANES)]
                    target = outs[k].at[pl.ds(j * tile, tile)]
                    copies.append(pltpu.make_async_copy(source, target, sems.at[k, j]))
                else:
                    outs[k][j * tile : (j + 1) * tile, :] = rows[pl.ds(start, tile), :]
        for copy in copies:
            copy.start()
        for n in range(len(carried)):
            refs[first_out + slab_count + n][...] = refs[part_count + n][...]
        for copy in copies:
            copy.wait()

    dtype = parts[0].dtype
    results = pl.pallas_call(
        kernel,
        in_specs=[HBM] + [HBM if whole else VMEM] * part_count + [VMEM] * len(carried),
        out_specs=[VMEM] * (slab_count + len(carried)),
        out_shape=[jax.ShapeDtypeStruct((listed * tile, LANES), dtype)] * slab_count
        + [jax.ShapeDtypeStruct(array.shape, array.dtype) for array in carried],
        scratch_shapes=[
            pltpu.SMEM(ref_table.shape, ref_table.dtype),
            pltpu.SemaphoreType.DMA(()),
            pltpu.VMEM((tile if whole else row_count, LANES), dtype),
            pltpu.SemaphoreType.DMA((slab_count, listed)),
        ],
        compiler_params=PARAMS,
        name="pick_tiles",
    )(ref_table, *parts, *carried)
    return results[:slab_count], results[slab_count:]


def convolve(arrived, tile_rows, tile_sources, tile_counts, tile_values, row_count, group):
    slab_count = len(arrived)
    piece, width = arrived[0].shape
    tile = tile_values.shape[2]
    group_rows = row_count // group

    tables = (tile_rows, tile_sources, tile_counts)

    slots = tile_values.shape[1]

    def kernel(*refs):
        pieces = refs[4 : 4 + slab_count]
        outs = refs[4 + slab_count : 4 + slab_count + group]
        rows, sources, counts, values, sems, inputs, total = refs[4 + slab_count + group :]
        slab = lax.axis_index("slab")
        _, _, lead = seat(group)
        fetches = [
            pltpu.make_async_copy(refs[n], local_ref, sems.at[n])
            for n, local_ref in enumerate((rows, sources, counts))
        ]
        batches = [
            pltpu.make_async_copy(
                refs[3].at[0, pl.ds(slot, BATCH)],
                values.at[pl.ds(slot, BATCH)],
                sems.at[3 + slot // BATCH],
            )
            for slot in range(0, slots, BATCH)
        ]
        for copy in fetches + batches:
            copy.start()
        for k in range(slab_count):
            start = pl.multiple_of((slab ^ k) * piece, piece)
            inputs[pl.ds(start, piece), :] = pieces[k][...]
        total[...] = jnp.zeros_like(total)
        for fetch in fetches:
            fetch.wait()
        count = counts[0, 0]
        products = []
        for slot in range(slots):
            if slot % BATCH == 0:
                batches[slot // BATCH].wait()
            start = pl.multiple_of(sources[0, slot] * tile, tile)
            product = jnp.dot(
                values[slot],
                inputs[pl.ds(start, tile), :],
                preferred_element_type=jnp.float32,
            )
            products.append(jnp.where(slot < count, product, 0.0))
        for slot in range(slots):
            target = pl.multiple_of(rows[0, slot] * tile, tile)
            total[pl.ds(target, tile), :] += products[slot]
        for k in range(group):
            start = pl.multiple_of((lead ^ k) * group_rows, group_rows)
            outs[k][...] = total[pl.ds(start, group_rows), :].astype(outs[k].dtype)

    dtype = arrived[0].dtype
    return pl.pallas_call(
        kernel,
        in_specs=[HBM] * 4 + [VMEM] * slab_count,
        out_specs=[VMEM] * group,
        out_shape=[jax.ShapeDtypeStruct((group_rows, width), dtype)] * group,
        scratch_shapes=[pltpu.SMEM(table.shape, table.dtype) for table in tables]
        + [
            pltpu.VMEM(tile_values.shape[1:], tile_values.dtype),
            pltpu.SemaphoreType.DMA((3 + slots // BATCH,)),
            pltpu.VMEM((slab_count * piece, width), dtype),
            pltpu.VMEM((row_count, width), jnp.float32),
        ],
        compiler_params=PARAMS,
        name="convolve",
    )(*tables, tile_values, *arrived)


def sigmoid(value):
    return 0.5 * jnp.tanh(0.5 * value) + 0.5


def pack(mixed):
    columns, group = len(mixed), len(mixed[0])
    rows, lanes = mixed[0][0].shape
    blocks = [part for column in mixed for part in column]
    size = rows // CHUNKS

    def kernel(*refs):
        _, place, _ = seat(group)
        for n in range(len(blocks)):
            first = n // group * lanes
            for chunk, out in enumerate(refs[len(blocks) :]):
                source = refs[n][chunk * size : (chunk + 1) * size, :]
                out[place ^ (n % group), :, first : first + lanes] = source

    out_shape = jax.ShapeDtypeStruct((group, size, columns * lanes), blocks[0].dtype)
    return list(pl.pallas_call(
        kernel,
        in_specs=[VMEM] * len(blocks),
        out_specs=[VMEM] * CHUNKS,
        out_shape=[out_shape] * CHUNKS,
        compiler_params=PARAMS,
        name="pack",
    )(*blocks))


def spread_into(outs, chunks, place, group):
    lanes = outs[0].shape[1]
    for n, out in enumerate(outs):
        first = n // group * lanes
        base = 0
        for chunk in chunks:
            size = chunk.shape[1]
            out[base : base + size, :] = chunk[place ^ (n % group), :, first : first + lanes]
            base += size


def spread(chunks, lanes):
    group, size, units = chunks[0].shape
    count = units // lanes * group

    def kernel(*refs):
        _, place, _ = seat(group)
        spread_into(refs[len(chunks) :], refs[: len(chunks)], place, group)

    results = pl.pallas_call(
        kernel,
        in_specs=[VMEM] * len(chunks),
        out_specs=[VMEM] * count,
        out_shape=[jax.ShapeDtypeStruct((size * len(chunks), lanes), chunks[0].dtype)] * count,
        compiler_params=PARAMS,
        name="spread",
    )(*chunks)
    return [results[n : n + group] for n in range(0, count, group)]


def project(mixed, layer, w_input, w_hidden, bias, mode, after):
    group, size, _ = mixed[0].shape
    gates = w_input.shape[2]
    count = len(mixed)

    def kernel(w_in, w_rec, gate_bias, *refs):
        outs = refs[count + 1 :]
        half, _, _ = seat(group)

        @only(mode, half)
        def _():
            outs[count][...] = w_rec[layer]
            for n in range(count):
                for time in range(group):
                    part = jnp.dot(
                        refs[n][time], w_in[layer], preferred_element_type=jnp.float32
                    )
                    outs[n][time] = part + gate_bias[layer : layer + 1, :]

    results = pl.pallas_call(
        kernel,
        in_specs=[VMEM] * (4 + count),
        out_specs=[VMEM] * (count + 1),
        out_shape=[jax.ShapeDtypeStruct((group, size, gates), jnp.float32)] * count
        + [jax.ShapeDtypeStruct(w_hidden.shape[1:], w_hidden.dtype)],
        compiler_params=PARAMS,
        name="project",
    )(w_input, w_hidden, bias, *mixed, after)
    return results[:count], results[count]


def recur_projected(projected, weights, state, mode):
    group, size, gates = projected.shape
    units = gates // 4

    def kernel(inputs, w_rec, start, states, memory):
        half, _, _ = seat(group)

        @only(mode, half)
        def _():
            memory[...] = start[1].astype(jnp.float32)
            hidden = start[0]
            for time in range(group):
                gate = inputs[time] + jnp.dot(
                    hidden, w_rec[...], preferred_element_type=jnp.float32
                )
                i, f, g, o = (gate[:, n * units : (n + 1) * units] for n in range(4))
                new = sigmoid(f) * memory[...] + sigmoid(i) * jnp.tanh(g)
                memory[...] = new
                states[time] = (sigmoid(o) * jnp.tanh(new)).astype(states.dtype)
                hidden = states[time]

    return pl.pallas_call(
        kernel,
        in_specs=[VMEM] * 3,
        out_specs=VMEM,
        out_shape=jax.ShapeDtypeStruct((group, size, units), state.dtype),
        scratch_shapes=[pltpu.VMEM((size, units), jnp.float32)],
        compiler_params=PARAMS,
        name="recur",
    )(projected, weights, state)


def recur(mixed, layer, w_input, w_hidden, bias, mode, state=None, keep=None, lanes=0):
    group, size, _ = mixed.shape
    units = w_hidden.shape[1]
    first = state is None
    operands = [mixed] + ([] if keep is None else [keep]) + ([] if first else [state])
    outputs = units // lanes * group if lanes else 1

    def kernel(w_in, w_rec_hbm, gate_bias, *refs):
        inputs = refs[0]
        start = refs[len(operands) - 1]
        outs = refs[len(operands) : len(operands) + outputs]
        w_rec, sem, memory = refs[-3:]
        states = refs[-4] if lanes else outs[0]
        half, place, _ = seat(group)

        if keep is not None:

            @pl.when(half != mode)
            def _():
                spread_into(outs, refs[1:2], place, group)

        @only(mode, half)
        def _():
            fetch = pltpu.make_async_copy(w_rec_hbm.at[layer], w_rec, sem)
            fetch.start()
            line = gate_bias[layer : layer + 1, :]

            def advance(gates, old, time):
                i, f, g, o = (gates[:, n * units : (n + 1) * units] for n in range(4))
                new = sigmoid(i) * jnp.tanh(g)
                if old is not None:
                    new = sigmoid(f) * old + new
                memory[...] = new
                states[time] = (sigmoid(o) * jnp.tanh(new)).astype(states.dtype)

            hidden = None if first else start[0]
            if not first:
                memory[...] = start[1].astype(jnp.float32)
            for time in range(group):
                gates = jnp.dot(inputs[time], w_in[layer], preferred_element_type=jnp.float32)
                gates = gates + line
                if time == (1 if first else 0):
                    fetch.wait()
                if hidden is not None:
                    gates = gates + jnp.dot(
                        hidden, w_rec[...], preferred_element_type=jnp.float32
                    )
                advance(gates, None if hidden is None else memory[...], time)
                hidden = states[time]
            if group == 1 and first:
                fetch.wait()
            if lanes:
                spread_into(outs, [states], place, group)
            if first:
                last = refs[len(operands) + outputs]
                last[0] = states[group - 1]
                last[1] = memory[...].astype(last.dtype)

        if first:
            side = refs[len(operands) + outputs + 1]
            side[...] = jnp.full(side.shape, half, side.dtype)

    dtype = mixed.dtype
    if lanes:
        out_shape = [jax.ShapeDtypeStruct((size, lanes), dtype)] * outputs
    else:
        out_shape = [jax.ShapeDtypeStruct((group, size, units), dtype)]
    if first:
        out_shape.append(jax.ShapeDtypeStruct((2, size, units), dtype))
        out_shape.append(jax.ShapeDtypeStruct((8, LANES), jnp.int32))
    results = pl.pallas_call(
        kernel,
        in_specs=[VMEM, HBM, VMEM] + [VMEM] * len(operands),
        out_specs=[VMEM] * len(out_shape),
        out_shape=out_shape,
        scratch_shapes=([pltpu.VMEM((group, size, units), dtype)] if lanes else [])
        + [
            pltpu.VMEM(w_hidden.shape[1:], w_hidden.dtype),
            pltpu.SemaphoreType.DMA(()),
            pltpu.VMEM((size, units), jnp.float32),
        ],
        compiler_params=PARAMS,
        name="recur",
    )(w_input, w_hidden, bias, *operands)
    if lanes:
        return [results[n : n + group] for n in range(0, outputs, group)]
    return results if first else results[0]


def assemble(parts):
    group = len(parts[0])
    size, width = parts[0][0].shape
    part_rows = size * len(parts)
    count = len(parts) * group

    def kernel(*refs):
        out, sems = refs[-2:]
        _, _, lead = seat(group)
        copies = []
        for n in range(count):
            start = (lead ^ (n % group)) * part_rows + n // group * size
            target = out.at[0, pl.ds(pl.multiple_of(start, size), size)]
            copies.append(pltpu.make_async_copy(refs[n], target, sems.at[n]))
        for copy in copies:
            copy.start()
        for copy in copies:
            copy.wait()

    return pl.pallas_call(
        kernel,
        in_specs=[VMEM] * count,
        out_specs=HBM,
        out_shape=jax.ShapeDtypeStruct((1, group * part_rows, width), parts[0][0].dtype),
        scratch_shapes=[pltpu.SemaphoreType.DMA((count,))],
        compiler_params=PARAMS,
        name="assemble",
    )(*(part for chunk in parts for part in chunk))


def send(array, target, lower_only=False):
    slab_count = lax.axis_size("slab")
    times = lax.axis_size("tm")
    pairs = []
    for time in range(times // 2 if lower_only else times):
        for slab in range(slab_count):
            to_time, to_slab = target(time, slab)
            pairs.append((time * slab_count + slab, to_time * slab_count + to_slab))
    return lax.ppermute(array, AXES, pairs)


def swap_slabs(arrays):
    got = list(arrays)
    for k in range(len(arrays) - 1, 0, -1):
        got[k] = send(arrays[k], lambda time, slab: (time, slab ^ k))
    return got


def swap_times(arrays):
    got = list(arrays)
    for k in range(len(arrays) - 1, 0, -1):
        got[k] = send(arrays[k], lambda time, slab: (time ^ k, slab))
    return got


def hand_over(last, group):
    flip = mirror(group)
    return send(last, lambda time, slab: (group + (time ^ flip), slab), lower_only=True)


def local(
    features, ref_lists, tile_rows, tile_sources, tile_counts, tile_values, w_input, w_hidden, bias
):
    row_count = features.shape[1]
    tile = tile_values.shape[2]
    slab_count = lax.axis_size("slab")
    layers = w_input.shape[0]
    group = lax.axis_size("tm") // 2

    def pick(parts, table, column=0, carried=()):
        return pick_tiles(parts, table, slab_count, row_count, tile, group, column, carried)

    def mix(listed):
        arrived = swap_slabs(listed)
        return swap_times(
            convolve(
                arrived, tile_rows, tile_sources, tile_counts, tile_values, row_count, group
            )
        )

    def back_and_mix(hidden):
        return pack([mix(pick(swap_times(column), table)[0]) for column in hidden])

    def run(mixed, layer, mode, *rest):
        return recur(mixed, layer, w_input, w_hidden, gate_bias, mode, *rest)

    def run_lower(mixed, layer):
        chunks, handed = [], []
        for part in mixed:
            states, last, side = run(part, layer, LOWER)
            handed.append(hand_over(last, group))
            chunks.append(states)
        return chunks, handed, side[0, 0]

    features = features[0]
    columns = features.shape[1] // LANES
    listed = [pick([features], ref_lists, column)[0] for column in range(columns - 1)]
    last, (table, gate_bias) = pick([features], ref_lists, columns - 1, (ref_lists, bias))
    upper_mixed = pack([mix(column) for column in [*listed, last]])
    hidden, handed, half = run_lower(upper_mixed, 0)
    for layer in range(1, layers):

        def lower_layer(hidden):
            return back_and_mix(spread(hidden, LANES))

        def upper_layer(states):
            return back_and_mix(spread(states, LANES))

        lower_mixed = lax.cond(half == LOWER, lower_layer, lambda hidden: hidden, hidden)
        hidden, following, half = run_lower(lower_mixed, layer)
        projected, recurrent = project(
            upper_mixed, layer - 1, w_input, w_hidden, gate_bias, UPPER, hidden[-1]
        )
        states = [
            recur_projected(part, recurrent, state, UPPER)
            for part, state in zip(projected, handed)
        ]
        upper_mixed = lax.cond(half == UPPER, upper_layer, lambda states: states, states)
        handed = following
    units = w_hidden.shape[1]
    parts = []
    for number, (part, state) in enumerate(zip(upper_mixed, handed)):
        (states,) = run(part, layers - 1, UPPER, state, hidden[number], units)
        parts.append(swap_times(states))
    return assemble(parts)


def solution(mesh):
    in_specs = (
        P("tm", "slab", None),
        P("tm", None, None),
        P("tm", "slab"),
        P("tm", "slab"),
        P("tm", "slab"),
        P("tm", "slab", None, None),
        P(),
        P(),
        P(),
    )
    out_specs = P("tm", "slab", None)
    return jax.shard_map(local, mesh=mesh, in_specs=in_specs, out_specs=out_specs, check_vma=False)
```

```python
import jax
import jax.numpy as jnp
from jax import lax
from jax.experimental import pallas as pl
from jax.experimental.pallas import tpu as pltpu
from jax.sharding import PartitionSpec as P


HBM = pl.BlockSpec(memory_space=pltpu.HBM)
VMEM = pl.BlockSpec(memory_space=pltpu.VMEM)
PARAMS = pltpu.CompilerParams(vmem_limit_bytes=16 * 2**20)
UNROLL = 32
LANES = 128
CHUNKS = 2
AXES = ("tm", "slab")
LOWER, UPPER, BOTH = 0, 1, None


def seat(group):
    index = lax.axis_index("tm")
    half = index // group
    place = index % group
    return half, place


def only(mode, half):
    def run(body):
        if mode is BOTH:
            body()
        else:
            pl.when(half == mode)(body)

    return run


def pick_tiles(parts, ref_table, slab_count, row_count, tile, group, column, carried=()):
    part_count = len(parts)
    part_rows = parts[0].shape[0]
    listed = ref_table.shape[2] // slab_count
    whole = part_count == 1

    def kernel(table_hbm, *refs):
        sources = refs[:part_count]
        first_out = part_count + len(carried)
        outs = refs[first_out : first_out + slab_count]
        table, table_sem, rows, sems = refs[-4:]
        slab = lax.axis_index("slab")
        _, place = seat(group)
        fetch = pltpu.make_async_copy(table_hbm, table, table_sem)
        fetch.start()
        if not whole:
            for k in range(part_count):
                start = pl.multiple_of((place ^ k) * part_rows, part_rows)
                rows[pl.ds(start, part_rows), :] = sources[k][...]
        fetch.wait()
        copies = []
        for k in reversed(range(slab_count)):
            for j in range(listed):
                index = table[0, slab ^ k, slab * listed + j]
                start = pl.multiple_of(index * tile, tile)
                if whole:
                    source = sources[0].at[pl.ds(start, tile), pl.ds(column * LANES, LANES)]
                    target = outs[k].at[pl.ds(j * tile, tile)]
                    copies.append(pltpu.make_async_copy(source, target, sems.at[k, j]))
                else:
                    outs[k][j * tile : (j + 1) * tile, :] = rows[pl.ds(start, tile), :]
        for copy in copies:
            copy.start()
        for n in range(len(carried)):
            refs[first_out + slab_count + n][...] = refs[part_count + n][...]
        for copy in copies:
            copy.wait()

    dtype = parts[0].dtype
    results = pl.pallas_call(
        kernel,
        in_specs=[HBM] + [HBM if whole else VMEM] * part_count + [VMEM] * len(carried),
        out_specs=[VMEM] * (slab_count + len(carried)),
        out_shape=[jax.ShapeDtypeStruct((listed * tile, LANES), dtype)] * slab_count
        + [jax.ShapeDtypeStruct(array.shape, array.dtype) for array in carried],
        scratch_shapes=[
            pltpu.SMEM(ref_table.shape, ref_table.dtype),
            pltpu.SemaphoreType.DMA(()),
            pltpu.VMEM((tile if whole else row_count, LANES), dtype),
            pltpu.SemaphoreType.DMA((slab_count, listed)),
        ],
        compiler_params=PARAMS,
        name="pick_tiles",
    )(ref_table, *parts, *carried)
    return results[:slab_count], results[slab_count:]


def convolve(arrived, tile_rows, tile_sources, tile_counts, tile_values, row_count, group):
    slab_count = len(arrived)
    piece, width = arrived[0].shape
    tile = tile_values.shape[2]
    group_rows = row_count // group

    tables = (tile_rows, tile_sources, tile_counts)
    unroll = min(UNROLL, tile_values.shape[1])

    def kernel(*refs):
        values = refs[3]
        pieces = refs[4 : 4 + slab_count]
        outs = refs[4 + slab_count : 4 + slab_count + group]
        rows, sources, counts, sems, inputs, total = refs[4 + slab_count + group :]
        slab = lax.axis_index("slab")
        _, place = seat(group)
        fetches = [
            pltpu.make_async_copy(refs[n], local_ref, sems.at[n])
            for n, local_ref in enumerate((rows, sources, counts))
        ]
        for fetch in fetches:
            fetch.start()
        for k in range(slab_count):
            start = pl.multiple_of((slab ^ k) * piece, piece)
            inputs[pl.ds(start, piece), :] = pieces[k][...]
        total[...] = jnp.zeros_like(total)
        for fetch in fetches:
            fetch.wait()
        count = counts[0, 0]

        def step(index, carry):
            products = []
            for lane in range(unroll):
                slot = index * unroll + lane
                start = pl.multiple_of(sources[0, slot] * tile, tile)
                product = jnp.dot(
                    values[0, slot],
                    inputs[pl.ds(start, tile), :],
                    preferred_element_type=jnp.float32,
                )
                products.append(jnp.where(slot < count, product, 0.0))
            for lane in range(unroll):
                target = pl.multiple_of(rows[0, index * unroll + lane] * tile, tile)
                total[pl.ds(target, tile), :] += products[lane]
            return carry

        lax.fori_loop(0, (count + unroll - 1) // unroll, step, 0)
        for k in range(group):
            start = pl.multiple_of((place ^ k) * group_rows, group_rows)
            outs[k][...] = total[pl.ds(start, group_rows), :].astype(outs[k].dtype)

    dtype = arrived[0].dtype
    return pl.pallas_call(
        kernel,
        in_specs=[HBM, HBM, HBM, VMEM] + [VMEM] * slab_count,
        out_specs=[VMEM] * group,
        out_shape=[jax.ShapeDtypeStruct((group_rows, width), dtype)] * group,
        scratch_shapes=[pltpu.SMEM(table.shape, table.dtype) for table in tables]
        + [
            pltpu.SemaphoreType.DMA((3,)),
            pltpu.VMEM((slab_count * piece, width), dtype),
            pltpu.VMEM((row_count, width), jnp.float32),
        ],
        compiler_params=PARAMS,
        name="convolve",
    )(*tables, tile_values, *arrived)


def sigmoid(value):
    return 0.5 * jnp.tanh(0.5 * value) + 0.5


def pack(mixed):
    columns, group = len(mixed), len(mixed[0])
    rows, lanes = mixed[0][0].shape
    blocks = [part for column in mixed for part in column]
    size = rows // CHUNKS

    def kernel(*refs):
        _, place = seat(group)
        for n in range(len(blocks)):
            first = n // group * lanes
            for chunk, out in enumerate(refs[len(blocks) :]):
                source = refs[n][chunk * size : (chunk + 1) * size, :]
                out[place ^ (n % group), :, first : first + lanes] = source

    out_shape = jax.ShapeDtypeStruct((group, size, columns * lanes), blocks[0].dtype)
    return list(pl.pallas_call(
        kernel,
        in_specs=[VMEM] * len(blocks),
        out_specs=[VMEM] * CHUNKS,
        out_shape=[out_shape] * CHUNKS,
        compiler_params=PARAMS,
        name="pack",
    )(*blocks))


def spread_into(outs, chunks, place, group):
    lanes = outs[0].shape[1]
    for n, out in enumerate(outs):
        first = n // group * lanes
        base = 0
        for chunk in chunks:
            size = chunk.shape[1]
            out[base : base + size, :] = chunk[place ^ (n % group), :, first : first + lanes]
            base += size


def spread(chunks, lanes):
    group, size, units = chunks[0].shape
    count = units // lanes * group

    def kernel(*refs):
        _, place = seat(group)
        spread_into(refs[len(chunks) :], refs[: len(chunks)], place, group)

    results = pl.pallas_call(
        kernel,
        in_specs=[VMEM] * len(chunks),
        out_specs=[VMEM] * count,
        out_shape=[jax.ShapeDtypeStruct((size * len(chunks), lanes), chunks[0].dtype)] * count,
        compiler_params=PARAMS,
        name="spread",
    )(*chunks)
    return [results[n : n + group] for n in range(0, count, group)]


def recur(mixed, layer, w_input, w_hidden, bias, mode, state=None, done=(), keep=(), lanes=0):
    group, size, _ = mixed.shape
    units = w_hidden.shape[1]
    first = state is None
    operands = [mixed] + list(done) + list(keep) + ([] if first else [state])
    outputs = units // lanes * group if lanes else 1

    def kernel(w_in, w_rec_hbm, gate_bias, *refs):
        inputs = refs[0]
        earlier = refs[1 : 1 + len(done)]
        kept = refs[1 + len(done) : 1 + len(done) + len(keep)]
        start = refs[len(operands) - 1]
        outs = refs[len(operands) : len(operands) + outputs]
        w_rec, sem, memory = refs[-3:]
        states = refs[-4] if lanes else outs[0]
        half, place = seat(group)

        if keep:

            @pl.when(half != mode)
            def _():
                spread_into(outs, kept, place, group)

        @only(mode, half)
        def _():
            fetch = pltpu.make_async_copy(w_rec_hbm.at[layer], w_rec, sem)
            fetch.start()
            line = gate_bias[layer : layer + 1, :]

            def advance(gates, old, time):
                i, f, g, o = (gates[:, n * units : (n + 1) * units] for n in range(4))
                new = sigmoid(i) * jnp.tanh(g)
                if old is not None:
                    new = sigmoid(f) * old + new
                memory[...] = new
                states[time] = (sigmoid(o) * jnp.tanh(new)).astype(states.dtype)

            hidden = None if first else start[0]
            if not first:
                memory[...] = start[1].astype(jnp.float32)
            for time in range(group):
                gates = jnp.dot(inputs[time], w_in[layer], preferred_element_type=jnp.float32)
                gates = gates + line
                if time == min(int(first), group - 1):
                    fetch.wait()
                if hidden is not None:
                    gates = gates + jnp.dot(
                        hidden, w_rec[...], preferred_element_type=jnp.float32
                    )
                advance(gates, None if hidden is None else memory[...], time)
                hidden = states[time]
            if lanes:
                spread_into(outs, [*earlier, states], place, group)
            if first:
                last = refs[len(operands) + outputs]
                last[0] = states[group - 1]
                last[1] = memory[...].astype(last.dtype)

    dtype = mixed.dtype
    if lanes:
        out_shape = [jax.ShapeDtypeStruct((size * (1 + len(done)), lanes), dtype)] * outputs
    else:
        out_shape = [jax.ShapeDtypeStruct((group, size, units), dtype)]
    if first:
        out_shape.append(jax.ShapeDtypeStruct((2, size, units), dtype))
    scratch = [pltpu.VMEM((group, size, units), dtype)] if lanes else []
    scratch += [pltpu.VMEM(w_hidden.shape[1:], w_hidden.dtype), pltpu.SemaphoreType.DMA(())]
    results = pl.pallas_call(
        kernel,
        in_specs=[VMEM, HBM, VMEM] + [VMEM] * len(operands),
        out_specs=[VMEM] * len(out_shape),
        out_shape=out_shape,
        scratch_shapes=scratch + [pltpu.VMEM((size, units), jnp.float32)],
        compiler_params=PARAMS,
        name="recur",
    )(w_input, w_hidden, bias, *operands)
    if lanes:
        return [results[n : n + group] for n in range(0, outputs, group)]
    return results if first else results[0]


def assemble(parts):
    group = len(parts[0])
    size, width = parts[0][0].shape
    part_rows = size * len(parts)
    count = len(parts) * group

    def kernel(*refs):
        out, sems = refs[-2:]
        _, place = seat(group)
        copies = []
        for n in range(count):
            start = (place ^ (n % group)) * part_rows + n // group * size
            target = out.at[0, pl.ds(pl.multiple_of(start, size), size)]
            copies.append(pltpu.make_async_copy(refs[n], target, sems.at[n]))
        for copy in copies:
            copy.start()
        for copy in copies:
            copy.wait()

    return pl.pallas_call(
        kernel,
        in_specs=[VMEM] * count,
        out_specs=HBM,
        out_shape=jax.ShapeDtypeStruct((1, group * part_rows, width), parts[0][0].dtype),
        scratch_shapes=[pltpu.SemaphoreType.DMA((count,))],
        compiler_params=PARAMS,
        name="assemble",
    )(*(part for chunk in parts for part in chunk))


def send(array, target, lower_only=False):
    slab_count = lax.axis_size("slab")
    times = lax.axis_size("tm")
    pairs = []
    for time in range(times // 2 if lower_only else times):
        for slab in range(slab_count):
            to_time, to_slab = target(time, slab)
            pairs.append((time * slab_count + slab, to_time * slab_count + to_slab))
    return lax.ppermute(array, AXES, pairs)


def swap_slabs(arrays):
    got = list(arrays)
    for k in range(len(arrays) - 1, 0, -1):
        got[k] = send(arrays[k], lambda time, slab: (time, slab ^ k))
    return got


def swap_times(arrays):
    got = list(arrays)
    for k in range(len(arrays) - 1, 0, -1):
        got[k] = send(arrays[k], lambda time, slab: (time ^ k, slab))
    return got


def hand_over(last, group):
    return send(last, lambda time, slab: (group + time, slab), lower_only=True)


def local(
    features, ref_lists, tile_rows, tile_sources, tile_counts, tile_values, w_input, w_hidden, bias
):
    row_count = features.shape[1]
    tile = tile_values.shape[2]
    slab_count = lax.axis_size("slab")
    layers = w_input.shape[0]
    group = lax.axis_size("tm") // 2
    half = lax.axis_index("tm") // group

    def pick(parts, table, column=0, carried=()):
        return pick_tiles(parts, table, slab_count, row_count, tile, group, column, carried)

    def mix(listed):
        arrived = swap_slabs(listed)
        return swap_times(
            convolve(
                arrived, tile_rows, tile_sources, tile_counts, tile_values, row_count, group
            )
        )

    def back_and_mix(hidden):
        return pack([mix(pick(swap_times(column), table)[0]) for column in hidden])

    def run(mixed, layer, mode, *rest):
        return recur(mixed, layer, w_input, w_hidden, gate_bias, mode, *rest)

    def run_lower(mixed, layer):
        chunks, handed = [], []
        for part in mixed:
            states, last = run(part, layer, LOWER)
            handed.append(hand_over(last, group))
            chunks.append(states)
        return chunks, handed

    def run_upper(mixed, layer, states):
        return [run(part, layer, UPPER, state) for part, state in zip(mixed[:-1], states)]

    features = features[0]
    columns = features.shape[1] // LANES
    listed = [pick([features], ref_lists, column)[0] for column in range(columns - 1)]
    last, (table, gate_bias) = pick([features], ref_lists, columns - 1, (ref_lists, bias))
    upper_mixed = pack([mix(column) for column in [*listed, last]])
    hidden, handed = run_lower(upper_mixed, 0)
    for layer in range(1, layers):

        def lower_layer(hidden):
            return back_and_mix(spread(hidden, LANES)), half + 1

        def upper_layer(mixed, done, state):
            return back_and_mix(run(mixed[-1], layer - 1, BOTH, state, done, (), LANES))

        lower_mixed, turn = lax.cond(
            half == LOWER, lower_layer, lambda hidden: (hidden, half), hidden
        )
        hidden, following = run_lower(lower_mixed, layer)
        done = run_upper(upper_mixed, layer - 1, handed)
        upper_mixed = lax.cond(
            half == turn,
            upper_layer,
            lambda mixed, done, state: mixed,
            upper_mixed,
            done,
            handed[-1],
        )
        handed = following
    units = w_hidden.shape[1]
    parts = []
    for number, (part, state) in enumerate(zip(upper_mixed, handed)):
        (states,) = run(part, layers - 1, UPPER, state, (), hidden[number : number + 1], units)
        parts.append(swap_times(states))
    return assemble(parts)


def solution(mesh):
    in_specs = (
        P("tm", "slab", None),
        P("tm", None, None),
        P("tm", "slab"),
        P("tm", "slab"),
        P("tm", "slab"),
        P("tm", "slab", None, None),
        P(),
        P(),
        P(),
    )
    out_specs = P("tm", "slab", None)
    return jax.shard_map(local, mesh=mesh, in_specs=in_specs, out_specs=out_specs, check_vma=False)
```

```python
import jax
import jax.numpy as jnp
from jax import lax
from jax.experimental import pallas as pl
from jax.experimental.pallas import tpu as pltpu
from jax.sharding import PartitionSpec as P


HBM = pl.BlockSpec(memory_space=pltpu.HBM)
VMEM = pl.BlockSpec(memory_space=pltpu.VMEM)
PARAMS = pltpu.CompilerParams(vmem_limit_bytes=16 * 2**20)
UNROLL = 32
LANES = 128
CHUNKS = 2
AXES = ("tm", "slab")
LOWER, UPPER, BOTH = 0, 1, None


def seat(group):
    index = lax.axis_index("tm")
    half = index // group
    place = index % group
    return half, place, place ^ (half * mirror(group))


def mirror(group):
    return group - 2 if group > 2 else 0


def only(mode, half):
    def run(body):
        if mode is BOTH:
            body()
        else:
            pl.when(half == mode)(body)

    return run


def pick_tiles(parts, ref_table, slab_count, row_count, tile, group, column, carried=()):
    part_count = len(parts)
    part_rows = parts[0].shape[0]
    listed = ref_table.shape[2] // slab_count
    whole = part_count == 1

    def kernel(table_hbm, *refs):
        sources = refs[:part_count]
        first_out = part_count + len(carried)
        outs = refs[first_out : first_out + slab_count]
        table, table_sem, rows, sems, carry_sems = refs[-5:]
        moves = [
            pltpu.make_async_copy(
                refs[part_count + n], refs[first_out + slab_count + n], carry_sems.at[n]
            )
            for n in range(len(carried))
        ]
        slab = lax.axis_index("slab")
        _, _, lead = seat(group)
        fetch = pltpu.make_async_copy(table_hbm, table, table_sem)
        fetch.start()
        if not whole:
            for k in range(part_count):
                start = pl.multiple_of((lead ^ k) * part_rows, part_rows)
                rows[pl.ds(start, part_rows), :] = sources[k][...]
        fetch.wait()
        copies = []
        for k in reversed(range(slab_count)):
            for j in range(listed):
                index = table[0, slab ^ k, slab * listed + j]
                start = pl.multiple_of(index * tile, tile)
                if whole:
                    source = sources[0].at[pl.ds(start, tile), pl.ds(column * LANES, LANES)]
                    target = outs[k].at[pl.ds(j * tile, tile)]
                    copies.append(pltpu.make_async_copy(source, target, sems.at[k, j]))
                else:
                    outs[k][j * tile : (j + 1) * tile, :] = rows[pl.ds(start, tile), :]
        copies += moves
        for copy in copies:
            copy.start()
        for copy in copies:
            copy.wait()

    dtype = parts[0].dtype
    results = pl.pallas_call(
        kernel,
        in_specs=[HBM] + [HBM if whole else VMEM] * part_count + [HBM] * len(carried),
        out_specs=[VMEM] * (slab_count + len(carried)),
        out_shape=[jax.ShapeDtypeStruct((listed * tile, LANES), dtype)] * slab_count
        + [jax.ShapeDtypeStruct(array.shape, array.dtype) for array in carried],
        scratch_shapes=[
            pltpu.SMEM(ref_table.shape, ref_table.dtype),
            pltpu.SemaphoreType.DMA(()),
            pltpu.VMEM((tile if whole else row_count, LANES), dtype),
            pltpu.SemaphoreType.DMA((slab_count, listed)),
            pltpu.SemaphoreType.DMA((max(len(carried), 1),)),
        ],
        compiler_params=PARAMS,
        name="pick_tiles",
    )(ref_table, *parts, *carried)
    return results[:slab_count], results[slab_count:]


def convolve(arrived, tile_rows, tile_sources, tile_counts, tile_values, row_count, group, chunks):
    slab_count = len(arrived)
    piece, width = arrived[0].shape
    tile = tile_values.shape[2]
    size = row_count // group // chunks
    count_out = group * chunks

    tables = (tile_rows, tile_sources, tile_counts)
    unroll = min(UNROLL, tile_values.shape[1])

    def kernel(*refs):
        values = refs[3]
        pieces = refs[4 : 4 + slab_count]
        outs = refs[4 + slab_count : 4 + slab_count + count_out]
        rows, sources, counts, sems, inputs, total = refs[4 + slab_count + count_out :]
        slab = lax.axis_index("slab")
        _, _, lead = seat(group)
        fetches = [
            pltpu.make_async_copy(refs[n], local_ref, sems.at[n])
            for n, local_ref in enumerate((rows, sources, counts))
        ]
        for fetch in fetches:
            fetch.start()
        for k in range(slab_count):
            start = pl.multiple_of((slab ^ k) * piece, piece)
            inputs[pl.ds(start, piece), :] = pieces[k][...]
        total[...] = jnp.zeros_like(total)
        for fetch in fetches:
            fetch.wait()
        count = counts[0, 0]

        def step(index, carry):
            products = []
            for lane in range(unroll):
                slot = index * unroll + lane
                start = pl.multiple_of(sources[0, slot] * tile, tile)
                product = jnp.dot(
                    values[0, slot],
                    inputs[pl.ds(start, tile), :],
                    preferred_element_type=jnp.float32,
                )
                products.append(jnp.where(slot < count, product, 0.0))
            for lane in range(unroll):
                target = pl.multiple_of(rows[0, index * unroll + lane] * tile, tile)
                total[pl.ds(target, tile), :] += products[lane]
            return carry

        lax.fori_loop(0, (count + unroll - 1) // unroll, step, 0)
        for n in range(count_out):
            start = (lead ^ (n % group)) * (size * chunks) + n // group * size
            rounded = total[pl.ds(pl.multiple_of(start, size), size), :]
            outs[n][...] = rounded.astype(outs[n].dtype)

    dtype = arrived[0].dtype
    results = pl.pallas_call(
        kernel,
        in_specs=[HBM, HBM, HBM, VMEM] + [VMEM] * slab_count,
        out_specs=[VMEM] * count_out,
        out_shape=[jax.ShapeDtypeStruct((size, width), dtype)] * count_out,
        scratch_shapes=[pltpu.SMEM(table.shape, table.dtype) for table in tables]
        + [
            pltpu.SemaphoreType.DMA((3,)),
            pltpu.VMEM((slab_count * piece, width), dtype),
            pltpu.VMEM((row_count, width), jnp.float32),
        ],
        compiler_params=PARAMS,
        name="convolve",
    )(*tables, tile_values, *arrived)
    return [results[n : n + group] for n in range(0, count_out, group)]


def sigmoid(value):
    return 0.5 * jnp.tanh(0.5 * value) + 0.5


def pack(mixed):
    columns, group = len(mixed), len(mixed[0])
    rows, lanes = mixed[0][0].shape
    blocks = [part for column in mixed for part in column]
    size = rows // CHUNKS

    def kernel(*refs):
        _, place, _ = seat(group)
        for n in range(len(blocks)):
            first = n // group * lanes
            for chunk, out in enumerate(refs[len(blocks) :]):
                source = refs[n][chunk * size : (chunk + 1) * size, :]
                out[place ^ (n % group), :, first : first + lanes] = source

    out_shape = jax.ShapeDtypeStruct((group, size, columns * lanes), blocks[0].dtype)
    return list(pl.pallas_call(
        kernel,
        in_specs=[VMEM] * len(blocks),
        out_specs=[VMEM] * CHUNKS,
        out_shape=[out_shape] * CHUNKS,
        compiler_params=PARAMS,
        name="pack",
    )(*blocks))


def pack_chunk(mixed, chunk):
    columns, group = len(mixed), len(mixed[0])
    size = min(column[0].shape[0] for column in mixed)
    lanes = mixed[0][0].shape[1]
    blocks = [part for column in mixed for part in column]

    def kernel(*refs):
        _, place, _ = seat(group)
        for n in range(len(blocks)):
            first = n // group * lanes
            base = chunk * size if blocks[n].shape[0] > size else 0
            source = refs[n][base : base + size, :]
            refs[-1][place ^ (n % group), :, first : first + lanes] = source

    return pl.pallas_call(
        kernel,
        in_specs=[VMEM] * len(blocks),
        out_specs=VMEM,
        out_shape=jax.ShapeDtypeStruct((group, size, columns * lanes), blocks[0].dtype),
        compiler_params=PARAMS,
        name="pack_chunk",
    )(*blocks)


def spread_into(outs, chunks, place, group):
    lanes = outs[0].shape[1]
    for n, out in enumerate(outs):
        first = n // group * lanes
        base = 0
        for chunk in chunks:
            size = chunk.shape[1]
            out[base : base + size, :] = chunk[place ^ (n % group), :, first : first + lanes]
            base += size


def spread(chunks, lanes):
    group, size, units = chunks[0].shape
    count = units // lanes * group

    def kernel(*refs):
        _, place, _ = seat(group)
        spread_into(refs[len(chunks) :], refs[: len(chunks)], place, group)

    results = pl.pallas_call(
        kernel,
        in_specs=[VMEM] * len(chunks),
        out_specs=[VMEM] * count,
        out_shape=[jax.ShapeDtypeStruct((size * len(chunks), lanes), chunks[0].dtype)] * count,
        compiler_params=PARAMS,
        name="spread",
    )(*chunks)
    return [results[n : n + group] for n in range(0, count, group)]


def recur(mixed, layer, w_input, w_hidden, bias, mode, state=None, done=(), keep=(), lanes=0):
    group, size, _ = mixed.shape
    units = w_hidden.shape[1]
    first = state is None
    operands = [mixed] + list(done) + list(keep) + ([] if first else [state])
    outputs = units // lanes * group if lanes else 1

    def kernel(w_in, w_rec, gate_bias, *refs):
        inputs = refs[0]
        earlier = refs[1 : 1 + len(done)]
        kept = refs[1 + len(done) : 1 + len(done) + len(keep)]
        start = refs[len(operands) - 1]
        outs = refs[len(operands) : len(operands) + outputs]
        memory = refs[-1]
        states = refs[-2] if lanes else outs[0]
        half, place, _ = seat(group)

        if keep:

            @pl.when(half != mode)
            def _():
                spread_into(outs, kept, place, group)

        @only(mode, half)
        def _():
            line = gate_bias[layer : layer + 1, :]

            def advance(gates, old, time):
                i, f, g, o = (gates[:, n * units : (n + 1) * units] for n in range(4))
                new = sigmoid(i) * jnp.tanh(g)
                if old is not None:
                    new = sigmoid(f) * old + new
                memory[...] = new
                states[time] = (sigmoid(o) * jnp.tanh(new)).astype(states.dtype)

            def project(time):
                return jnp.dot(inputs[time], w_in[layer], preferred_element_type=jnp.float32) + line

            def step(time, hidden):
                gates = project(time) + jnp.dot(
                    hidden, w_rec[layer], preferred_element_type=jnp.float32
                )
                advance(gates, memory[...], time)

            if first:
                advance(project(0), None, 0)
            else:
                memory[...] = start[1].astype(jnp.float32)
                step(0, start[0])

            def loop(time, carry):
                step(time, states[time - 1])
                return carry

            lax.fori_loop(1, group, loop, 0, unroll=True)
            if lanes:
                spread_into(outs, [*earlier, states], place, group)
            if first:
                last = refs[len(operands) + outputs]
                last[0] = states[group - 1]
                last[1] = memory[...].astype(last.dtype)

    dtype = mixed.dtype
    if lanes:
        out_shape = [jax.ShapeDtypeStruct((size * (1 + len(done)), lanes), dtype)] * outputs
    else:
        out_shape = [jax.ShapeDtypeStruct((group, size, units), dtype)]
    if first:
        out_shape.append(jax.ShapeDtypeStruct((2, size, units), dtype))
    scratch = [pltpu.VMEM((group, size, units), dtype)] if lanes else []
    results = pl.pallas_call(
        kernel,
        in_specs=[VMEM] * (3 + len(operands)),
        out_specs=[VMEM] * len(out_shape),
        out_shape=out_shape,
        scratch_shapes=scratch + [pltpu.VMEM((size, units), jnp.float32)],
        compiler_params=PARAMS,
        name="recur",
    )(w_input, w_hidden, bias, *operands)
    if lanes:
        return [results[n : n + group] for n in range(0, outputs, group)]
    return results if first else results[0]


def assemble(parts):
    group = len(parts[0])
    size, width = parts[0][0].shape
    part_rows = size * len(parts)
    count = len(parts) * group

    def kernel(*refs):
        out, sems = refs[-2:]
        _, _, lead = seat(group)
        copies = []
        for n in range(count):
            start = (lead ^ (n % group)) * part_rows + n // group * size
            target = out.at[0, pl.ds(pl.multiple_of(start, size), size)]
            copies.append(pltpu.make_async_copy(refs[n], target, sems.at[n]))
        for copy in copies:
            copy.start()
        for copy in copies:
            copy.wait()

    return pl.pallas_call(
        kernel,
        in_specs=[VMEM] * count,
        out_specs=HBM,
        out_shape=jax.ShapeDtypeStruct((1, group * part_rows, width), parts[0][0].dtype),
        scratch_shapes=[pltpu.SemaphoreType.DMA((count,))],
        compiler_params=PARAMS,
        name="assemble",
    )(*(part for chunk in parts for part in chunk))


def send(array, target, lower_only=False):
    slab_count = lax.axis_size("slab")
    times = lax.axis_size("tm")
    pairs = []
    for time in range(times // 2 if lower_only else times):
        for slab in range(slab_count):
            to_time, to_slab = target(time, slab)
            pairs.append((time * slab_count + slab, to_time * slab_count + to_slab))
    return lax.ppermute(array, AXES, pairs)


def swap_slabs(arrays):
    got = list(arrays)
    for k in range(len(arrays) - 1, 0, -1):
        got[k] = send(arrays[k], lambda time, slab: (time, slab ^ k))
    return got


def swap_times(arrays):
    got = list(arrays)
    for k in range(len(arrays) - 1, 0, -1):
        got[k] = send(arrays[k], lambda time, slab: (time ^ k, slab))
    return got


def hand_over(last, group):
    flip = mirror(group)
    return send(last, lambda time, slab: (group + (time ^ flip), slab), lower_only=True)


def local(
    features, ref_lists, tile_rows, tile_sources, tile_counts, tile_values, w_input, w_hidden, bias
):
    row_count = features.shape[1]
    tile = tile_values.shape[2]
    slab_count = lax.axis_size("slab")
    layers = w_input.shape[0]
    group = lax.axis_size("tm") // 2
    half = lax.axis_index("tm") // group

    def pick(parts, table, column=0, carried=()):
        return pick_tiles(parts, table, slab_count, row_count, tile, group, column, carried)

    def mix(listed, chunks=1):
        arrived = swap_slabs(listed)
        mixed = convolve(
            arrived, tile_rows, tile_sources, tile_counts, tile_values, row_count, group, chunks
        )
        got = []
        for part in mixed:
            got.append(swap_times(part))
        return got if chunks > 1 else got[0]

    def back_and_mix(hidden):
        return pack([mix(pick(swap_times(column), table)[0]) for column in hidden])

    def run(mixed, layer, mode, *rest):
        return recur(mixed, layer, w_input, w_hidden, gate_bias, mode, *rest)

    def run_lower(mixed, layer):
        chunks, handed = [], []
        for part in mixed:
            states, last = run(part, layer, LOWER)
            handed.append(hand_over(last, group))
            chunks.append(states)
        return chunks, handed

    def run_upper(mixed, layer, states):
        return [run(part, layer, UPPER, state) for part, state in zip(mixed[:-1], states)]

    features = features[0]
    columns = features.shape[1] // LANES
    listed = [pick([features], ref_lists, column)[0] for column in range(columns - 1)]
    last, (table, gate_bias) = pick([features], ref_lists, columns - 1, (ref_lists, bias))
    early = [mix(column) for column in listed]
    upper_mixed = [
        pack_chunk([*early, part], chunk) for chunk, part in enumerate(mix(last, CHUNKS))
    ]
    hidden, handed = run_lower(upper_mixed, 0)
    for layer in range(1, layers):

        def lower_layer(hidden):
            return back_and_mix(spread(hidden, LANES)), half + 1

        def upper_layer(mixed, done, state):
            return back_and_mix(run(mixed[-1], layer - 1, BOTH, state, done, (), LANES))

        lower_mixed, turn = lax.cond(
            half == LOWER, lower_layer, lambda hidden: (hidden, half), hidden
        )
        hidden, following = run_lower(lower_mixed, layer)
        done = run_upper(upper_mixed, layer - 1, handed)
        upper_mixed = lax.cond(
            half == turn,
            upper_layer,
            lambda mixed, done, state: mixed,
            upper_mixed,
            done,
            handed[-1],
        )
        handed = following
    units = w_hidden.shape[1]
    parts = []
    for number, (part, state) in enumerate(zip(upper_mixed, handed)):
        (states,) = run(part, layers - 1, UPPER, state, (), hidden[number : number + 1], units)
        parts.append(swap_times(states))
    return assemble(parts)


def solution(mesh):
    in_specs = (
        P("tm", "slab", None),
        P("tm", None, None),
        P("tm", "slab"),
        P("tm", "slab"),
        P("tm", "slab"),
        P("tm", "slab", None, None),
        P(),
        P(),
        P(),
    )
    out_specs = P("tm", "slab", None)
    return jax.shard_map(local, mesh=mesh, in_specs=in_specs, out_specs=out_specs, check_vma=False)
```

```python
import jax
import jax.numpy as jnp
from jax import lax
from jax.experimental import pallas as pl
from jax.experimental.pallas import tpu as pltpu
from jax.sharding import PartitionSpec as P


HBM = pl.BlockSpec(memory_space=pltpu.HBM)
VMEM = pl.BlockSpec(memory_space=pltpu.VMEM)
PARAMS = pltpu.CompilerParams(vmem_limit_bytes=16 * 2**20)
UNROLL = 32
LANES = 128
CHUNKS = 2
AXES = ("tm", "slab")
LOWER, UPPER, BOTH = 0, 1, None


def seat(group):
    index = lax.axis_index("tm")
    half = index // group
    place = index % group
    return half, place, place ^ (half * mirror(group))


def mirror(group):
    return group - 2 if group > 2 else 0


def only(mode, half):
    def run(body):
        if mode is BOTH:
            body()
        else:
            pl.when(half == mode)(body)

    return run


def pick_tiles(
    parts, ref_table, slab_count, row_count, tile, group, column, carried=(), scalars=()
):
    part_count = len(parts)
    part_rows = parts[0].shape[0]
    listed = ref_table.shape[2] // slab_count
    whole = part_count == 1

    def kernel(table_hbm, *refs):
        sources = refs[:part_count]
        first_out = part_count + len(carried) + len(scalars)
        outs = refs[first_out : first_out + slab_count]
        table, table_sem, rows, sems, carry_sems, numbers, number_sems = refs[-7:]
        last_out = first_out + slab_count + len(carried)
        loads = [
            pltpu.make_async_copy(
                refs[part_count + len(carried) + n], numbers.at[pl.ds(n, 1)], number_sems.at[n]
            )
            for n in range(len(scalars))
        ]
        for load in loads:
            load.start()
        moves = [
            pltpu.make_async_copy(
                refs[part_count + n], refs[first_out + slab_count + n], carry_sems.at[n]
            )
            for n in range(len(carried))
        ]
        slab = lax.axis_index("slab")
        _, _, lead = seat(group)
        fetch = pltpu.make_async_copy(table_hbm, table, table_sem)
        fetch.start()
        if not whole:
            for k in range(part_count):
                start = pl.multiple_of((lead ^ k) * part_rows, part_rows)
                rows[pl.ds(start, part_rows), :] = sources[k][...]
        fetch.wait()
        copies = []
        for k in reversed(range(slab_count)):
            for j in range(listed):
                index = table[0, slab ^ k, slab * listed + j]
                start = pl.multiple_of(index * tile, tile)
                if whole:
                    source = sources[0].at[pl.ds(start, tile), pl.ds(column * LANES, LANES)]
                    target = outs[k].at[pl.ds(j * tile, tile)]
                    copies.append(pltpu.make_async_copy(source, target, sems.at[k, j]))
                else:
                    outs[k][j * tile : (j + 1) * tile, :] = rows[pl.ds(start, tile), :]
        copies += moves
        for copy in copies:
            copy.start()
        for n, load in enumerate(loads):
            load.wait()
            spot = refs[last_out + n]
            spot[...] = jnp.full(spot.shape, numbers[n, 0], spot.dtype)
        for copy in copies:
            copy.wait()

    dtype = parts[0].dtype
    results = pl.pallas_call(
        kernel,
        in_specs=[HBM] + [HBM if whole else VMEM] * part_count + [HBM] * (len(carried) + len(scalars)),
        out_specs=[VMEM] * (slab_count + len(carried) + len(scalars)),
        out_shape=[jax.ShapeDtypeStruct((listed * tile, LANES), dtype)] * slab_count
        + [jax.ShapeDtypeStruct(array.shape, array.dtype) for array in carried]
        + [jax.ShapeDtypeStruct((8, LANES), array.dtype) for array in scalars],
        scratch_shapes=[
            pltpu.SMEM(ref_table.shape, ref_table.dtype),
            pltpu.SemaphoreType.DMA(()),
            pltpu.VMEM((tile if whole else row_count, LANES), dtype),
            pltpu.SemaphoreType.DMA((slab_count, listed)),
            pltpu.SemaphoreType.DMA((max(len(carried), 1),)),
            pltpu.SMEM((max(len(scalars), 1), 1), jnp.int32),
            pltpu.SemaphoreType.DMA((max(len(scalars), 1),)),
        ],
        compiler_params=PARAMS,
        name="pick_tiles",
    )(ref_table, *parts, *carried, *scalars)
    return results[:slab_count], results[slab_count:]


def convolve(arrived, tile_rows, tile_sources, tile_counts, tile_values, row_count, group, chunks):
    slab_count = len(arrived)
    piece, width = arrived[0].shape
    tile = tile_values.shape[2]
    size = row_count // group // chunks
    count_out = group * chunks

    tables = (tile_rows, tile_sources, tile_counts)
    unroll = min(UNROLL, tile_values.shape[1])

    def kernel(*refs):
        values = refs[3]
        pieces = refs[4 : 4 + slab_count]
        outs = refs[4 + slab_count : 4 + slab_count + count_out]
        rows, sources, counts, sems, inputs, total = refs[4 + slab_count + count_out :]
        slab = lax.axis_index("slab")
        _, _, lead = seat(group)
        fetches = [
            pltpu.make_async_copy(refs[n], local_ref, sems.at[n])
            for n, local_ref in enumerate((rows, sources, counts))
        ]
        for fetch in fetches:
            fetch.start()
        for k in range(slab_count):
            start = pl.multiple_of((slab ^ k) * piece, piece)
            inputs[pl.ds(start, piece), :] = pieces[k][...]
        total[...] = jnp.zeros_like(total)
        for fetch in fetches:
            fetch.wait()
        count = counts[0, 0]

        def step(index, carry):
            products = []
            for lane in range(unroll):
                slot = index * unroll + lane
                start = pl.multiple_of(sources[0, slot] * tile, tile)
                product = jnp.dot(
                    values[0, slot],
                    inputs[pl.ds(start, tile), :],
                    preferred_element_type=jnp.float32,
                )
                products.append(jnp.where(slot < count, product, 0.0))
            for lane in range(unroll):
                target = pl.multiple_of(rows[0, index * unroll + lane] * tile, tile)
                total[pl.ds(target, tile), :] += products[lane]
            return carry

        lax.fori_loop(0, (count + unroll - 1) // unroll, step, 0)
        for n in range(count_out):
            start = (lead ^ (n % group)) * (size * chunks) + n // group * size
            rounded = total[pl.ds(pl.multiple_of(start, size), size), :]
            outs[n][...] = rounded.astype(outs[n].dtype)

    dtype = arrived[0].dtype
    results = pl.pallas_call(
        kernel,
        in_specs=[HBM, HBM, HBM, VMEM] + [VMEM] * slab_count,
        out_specs=[VMEM] * count_out,
        out_shape=[jax.ShapeDtypeStruct((size, width), dtype)] * count_out,
        scratch_shapes=[pltpu.SMEM(table.shape, table.dtype) for table in tables]
        + [
            pltpu.SemaphoreType.DMA((3,)),
            pltpu.VMEM((slab_count * piece, width), dtype),
            pltpu.VMEM((row_count, width), jnp.float32),
        ],
        compiler_params=PARAMS,
        name="convolve",
    )(*tables, tile_values, *arrived)
    return [results[n : n + group] for n in range(0, count_out, group)]


def sigmoid(value):
    return 0.5 * jnp.tanh(0.5 * value) + 0.5


def pack(mixed):
    columns, group = len(mixed), len(mixed[0])
    rows, lanes = mixed[0][0].shape
    blocks = [part for column in mixed for part in column]
    size = rows // CHUNKS

    def kernel(*refs):
        _, place, _ = seat(group)
        for n in range(len(blocks)):
            first = n // group * lanes
            for chunk, out in enumerate(refs[len(blocks) :]):
                source = refs[n][chunk * size : (chunk + 1) * size, :]
                out[place ^ (n % group), :, first : first + lanes] = source

    out_shape = jax.ShapeDtypeStruct((group, size, columns * lanes), blocks[0].dtype)
    return list(pl.pallas_call(
        kernel,
        in_specs=[VMEM] * len(blocks),
        out_specs=[VMEM] * CHUNKS,
        out_shape=[out_shape] * CHUNKS,
        compiler_params=PARAMS,
        name="pack",
    )(*blocks))


def pack_chunk(mixed, chunk):
    columns, group = len(mixed), len(mixed[0])
    size = min(column[0].shape[0] for column in mixed)
    lanes = mixed[0][0].shape[1]
    blocks = [part for column in mixed for part in column]

    def kernel(*refs):
        _, place, _ = seat(group)
        for n in range(len(blocks)):
            first = n // group * lanes
            base = chunk * size if blocks[n].shape[0] > size else 0
            source = refs[n][base : base + size, :]
            refs[-1][place ^ (n % group), :, first : first + lanes] = source

    return pl.pallas_call(
        kernel,
        in_specs=[VMEM] * len(blocks),
        out_specs=VMEM,
        out_shape=jax.ShapeDtypeStruct((group, size, columns * lanes), blocks[0].dtype),
        compiler_params=PARAMS,
        name="pack_chunk",
    )(*blocks)


def spread_into(outs, chunks, place, group):
    lanes = outs[0].shape[1]
    for n, out in enumerate(outs):
        first = n // group * lanes
        base = 0
        for chunk in chunks:
            size = chunk.shape[1]
            out[base : base + size, :] = chunk[place ^ (n % group), :, first : first + lanes]
            base += size


def spread(chunks, lanes):
    group, size, units = chunks[0].shape
    count = units // lanes * group

    def kernel(*refs):
        _, place, _ = seat(group)
        spread_into(refs[len(chunks) :], refs[: len(chunks)], place, group)

    results = pl.pallas_call(
        kernel,
        in_specs=[VMEM] * len(chunks),
        out_specs=[VMEM] * count,
        out_shape=[jax.ShapeDtypeStruct((size * len(chunks), lanes), chunks[0].dtype)] * count,
        compiler_params=PARAMS,
        name="spread",
    )(*chunks)
    return [results[n : n + group] for n in range(0, count, group)]


def recur(mixed, layer, w_input, w_hidden, bias, mode, state=None, done=(), keep=(), lanes=0):
    group, size, _ = mixed.shape
    units = w_hidden.shape[1]
    first = state is None
    operands = [mixed] + list(done) + list(keep) + ([] if first else [state])
    outputs = units // lanes * group if lanes else 1

    def kernel(w_in, w_rec, gate_bias, *refs):
        inputs = refs[0]
        earlier = refs[1 : 1 + len(done)]
        kept = refs[1 + len(done) : 1 + len(done) + len(keep)]
        start = refs[len(operands) - 1]
        outs = refs[len(operands) : len(operands) + outputs]
        memory = refs[-1]
        states = refs[-2] if lanes else outs[0]
        half, place, _ = seat(group)

        if keep:

            @pl.when(half != mode)
            def _():
                spread_into(outs, kept, place, group)

        @only(mode, half)
        def _():
            line = gate_bias[layer : layer + 1, :]

            def advance(gates, old, time):
                i, f, g, o = (gates[:, n * units : (n + 1) * units] for n in range(4))
                new = sigmoid(i) * jnp.tanh(g)
                if old is not None:
                    new = sigmoid(f) * old + new
                memory[...] = new
                states[time] = (sigmoid(o) * jnp.tanh(new)).astype(states.dtype)

            def project(time):
                return jnp.dot(inputs[time], w_in[layer], preferred_element_type=jnp.float32) + line

            def step(time, hidden):
                gates = project(time) + jnp.dot(
                    hidden, w_rec[layer], preferred_element_type=jnp.float32
                )
                advance(gates, memory[...], time)

            if first:
                advance(project(0), None, 0)
            else:
                memory[...] = start[1].astype(jnp.float32)
                step(0, start[0])

            def loop(time, carry):
                step(time, states[time - 1])
                return carry

            lax.fori_loop(1, group, loop, 0, unroll=True)
            if lanes:
                spread_into(outs, [*earlier, states], place, group)
            if first:
                last = refs[len(operands) + outputs]
                last[0] = states[group - 1]
                last[1] = memory[...].astype(last.dtype)

    dtype = mixed.dtype
    if lanes:
        out_shape = [jax.ShapeDtypeStruct((size * (1 + len(done)), lanes), dtype)] * outputs
    else:
        out_shape = [jax.ShapeDtypeStruct((group, size, units), dtype)]
    if first:
        out_shape.append(jax.ShapeDtypeStruct((2, size, units), dtype))
    scratch = [pltpu.VMEM((group, size, units), dtype)] if lanes else []
    results = pl.pallas_call(
        kernel,
        in_specs=[VMEM] * (3 + len(operands)),
        out_specs=[VMEM] * len(out_shape),
        out_shape=out_shape,
        scratch_shapes=scratch + [pltpu.VMEM((size, units), jnp.float32)],
        compiler_params=PARAMS,
        name="recur",
    )(w_input, w_hidden, bias, *operands)
    if lanes:
        return [results[n : n + group] for n in range(0, outputs, group)]
    return results if first else results[0]


def assemble(parts):
    group = len(parts[0])
    size, width = parts[0][0].shape
    part_rows = size * len(parts)
    count = len(parts) * group

    def kernel(*refs):
        out, sems = refs[-2:]
        _, _, lead = seat(group)
        copies = []
        for n in range(count):
            start = (lead ^ (n % group)) * part_rows + n // group * size
            target = out.at[0, pl.ds(pl.multiple_of(start, size), size)]
            copies.append(pltpu.make_async_copy(refs[n], target, sems.at[n]))
        for copy in copies:
            copy.start()
        for copy in copies:
            copy.wait()

    return pl.pallas_call(
        kernel,
        in_specs=[VMEM] * count,
        out_specs=HBM,
        out_shape=jax.ShapeDtypeStruct((1, group * part_rows, width), parts[0][0].dtype),
        scratch_shapes=[pltpu.SemaphoreType.DMA((count,))],
        compiler_params=PARAMS,
        name="assemble",
    )(*(part for chunk in parts for part in chunk))


def send(array, target, lower_only=False):
    slab_count = lax.axis_size("slab")
    times = lax.axis_size("tm")
    pairs = []
    for time in range(times // 2 if lower_only else times):
        for slab in range(slab_count):
            to_time, to_slab = target(time, slab)
            pairs.append((time * slab_count + slab, to_time * slab_count + to_slab))
    return lax.ppermute(array, AXES, pairs)


def swap_slabs(arrays):
    got = list(arrays)
    for k in range(len(arrays) - 1, 0, -1):
        got[k] = send(arrays[k], lambda time, slab: (time, slab ^ k))
    return got


def swap_times(arrays):
    got = list(arrays)
    for k in range(len(arrays) - 1, 0, -1):
        got[k] = send(arrays[k], lambda time, slab: (time ^ k, slab))
    return got


def hand_over(last, group):
    flip = mirror(group)
    return send(last, lambda time, slab: (group + (time ^ flip), slab), lower_only=True)


def local(
    features, ref_lists, tile_rows, tile_sources, tile_counts, tile_values, w_input, w_hidden, bias
):
    row_count = features.shape[1]
    tile = tile_values.shape[2]
    slab_count = lax.axis_size("slab")
    layers = w_input.shape[0]
    group = lax.axis_size("tm") // 2
    half = lax.axis_index("tm") // group

    def pick(parts, table, column=0, *carried):
        return pick_tiles(parts, table, slab_count, row_count, tile, group, column, *carried)

    def mix(listed, live, chunks=1):
        arrived = swap_slabs(listed)
        mixed = convolve(
            arrived, tile_rows, tile_sources, live, tile_values, row_count, group, chunks
        )
        got = []
        for part in mixed:
            got.append(swap_times(part))
        return got if chunks > 1 else got[0]

    def back_and_mix(hidden):
        return pack([mix(pick(swap_times(column), table)[0], counts) for column in hidden])

    def run(mixed, layer, mode, *rest):
        return recur(mixed, layer, w_input, w_hidden, gate_bias, mode, *rest)

    def run_lower(mixed, layer):
        chunks, handed = [], []
        for part in mixed:
            states, last = run(part, layer, LOWER)
            handed.append(hand_over(last, group))
            chunks.append(states)
        return chunks, handed

    def run_upper(mixed, layer, states):
        return [run(part, layer, UPPER, state) for part, state in zip(mixed[:-1], states)]

    features = features[0]
    columns = features.shape[1] // LANES
    listed = [pick([features], ref_lists, column)[0] for column in range(columns - 1)]
    last, (table, gate_bias, counts) = pick(
        [features], ref_lists, columns - 1, (ref_lists, bias), (tile_counts,)
    )
    early = [mix(column, tile_counts) for column in listed]
    upper_mixed = [
        pack_chunk([*early, part], chunk) for chunk, part in enumerate(mix(last, tile_counts, CHUNKS))
    ]
    hidden, handed = run_lower(upper_mixed, 0)
    for layer in range(1, layers):

        def lower_layer(hidden):
            return back_and_mix(spread(hidden, LANES)), half + 1

        def upper_layer(mixed, done, state):
            return back_and_mix(run(mixed[-1], layer - 1, BOTH, state, done, (), LANES))

        lower_mixed, turn = lax.cond(
            half == LOWER, lower_layer, lambda hidden: (hidden, half), hidden
        )
        hidden, following = run_lower(lower_mixed, layer)
        done = run_upper(upper_mixed, layer - 1, handed)
        upper_mixed = lax.cond(
            half == turn,
            upper_layer,
            lambda mixed, done, state: mixed,
            upper_mixed,
            done,
            handed[-1],
        )
        handed = following
    units = w_hidden.shape[1]
    parts = []
    for number, (part, state) in enumerate(zip(upper_mixed, handed)):
        (states,) = run(part, layers - 1, UPPER, state, (), hidden[number : number + 1], units)
        parts.append(swap_times(states))
    return assemble(parts)


def solution(mesh):
    in_specs = (
        P("tm", "slab", None),
        P("tm", None, None),
        P("tm", "slab"),
        P("tm", "slab"),
        P("tm", "slab"),
        P("tm", "slab", None, None),
        P(),
        P(),
        P(),
    )
    out_specs = P("tm", "slab", None)
    return jax.shard_map(local, mesh=mesh, in_specs=in_specs, out_specs=out_specs, check_vma=False)
```

```python
import jax
import jax.numpy as jnp
from jax import lax
from jax.experimental import pallas as pl
from jax.experimental.pallas import tpu as pltpu
from jax.sharding import PartitionSpec as P


HBM = pl.BlockSpec(memory_space=pltpu.HBM)
SMEM = pl.BlockSpec(memory_space=pltpu.SMEM)
VMEM = pl.BlockSpec(memory_space=pltpu.VMEM)
PARAMS = pltpu.CompilerParams(vmem_limit_bytes=16 * 2**20)
UNROLL = 32
LANES = 128
CHUNKS = 2
AXES = ("tm", "slab")
LOWER, UPPER, BOTH = 0, 1, None


def seat(group):
    index = lax.axis_index("tm")
    half = index // group
    place = index % group
    return half, place, place ^ (half * mirror(group))


def mirror(group):
    return group - 2 if group > 2 else 0


def only(mode, half):
    def run(body):
        if mode is BOTH:
            body()
        else:
            pl.when(half == mode)(body)

    return run


def pick_tiles(
    parts, ref_table, list_length, slab_count, row_count, tile, group, carried=(), scalars=()
):
    part_count = len(parts)
    part_rows = parts[0].shape[0]
    whole = part_count == 1
    entries = ref_table.shape[2] if whole else ref_table.shape[1]
    listed = list_length
    emit = whole and len(scalars) > 0
    columns = parts[0].shape[1] // LANES
    picked = columns * slab_count
    matrix_shape = (pl.cdiv(slab_count, 8) * 8, pl.cdiv(entries, LANES) * LANES)

    def kernel(table_hbm, *refs):
        sources = refs[:part_count]
        first_out = part_count + len(carried) + len(scalars)
        outs = refs[first_out : first_out + picked]
        table, table_sem, rows, sems, carry_sems, numbers, number_sems = refs[-7:]
        last_out = first_out + picked + len(carried)
        loads = [
            pltpu.make_async_copy(
                refs[part_count + len(carried) + n], numbers.at[pl.ds(n, 1)], number_sems.at[n]
            )
            for n in range(len(scalars))
        ]
        for load in loads:
            load.start()
        moves = [
            pltpu.make_async_copy(
                refs[part_count + n], refs[first_out + picked + n], carry_sems.at[n]
            )
            for n in range(len(carried))
        ]
        slab = lax.axis_index("slab")
        _, _, lead = seat(group)
        if whole:
            table = table_hbm
        else:
            fetch = pltpu.make_async_copy(table_hbm, table, table_sem)
            fetch.start()
            for k in range(part_count):
                start = pl.multiple_of((lead ^ k) * part_rows, part_rows)
                rows[pl.ds(start, part_rows), :] = sources[k][...]
            fetch.wait()
        copies = []
        for k in reversed(range(slab_count)):
            for j in range(listed):
                spot = (slab ^ k, slab * listed + j)
                index = table[(0, *spot) if whole else spot]
                start = pl.multiple_of(index * tile, tile)
                for column in range(columns):
                    out = outs[column * slab_count + k]
                    lanes = pl.ds(column * LANES, LANES)
                    if whole:
                        copies.append(
                            pltpu.make_async_copy(
                                sources[0].at[pl.ds(start, tile), lanes],
                                out.at[pl.ds(j * tile, tile)],
                                sems.at[column * slab_count + k, j],
                            )
                        )
                    else:
                        out[j * tile : (j + 1) * tile, :] = rows[pl.ds(start, tile), lanes]
        copies += moves
        for copy in copies:
            copy.start()
        for n, load in enumerate(loads):
            load.wait()
            spread_out = refs[last_out + n]
            spread_out[...] = jnp.full(spread_out.shape, numbers[n, 0], jnp.int32)
        if emit:
            matrix = refs[last_out + len(scalars)]
            row = lax.broadcasted_iota(jnp.int32, matrix.shape, 0)
            lane = lax.broadcasted_iota(jnp.int32, matrix.shape, 1)
            filled = jnp.zeros(matrix.shape, jnp.int32)
            for p in range(slab_count):
                for j in range(entries):
                    filled = jnp.where((row == p) & (lane == j), table[0, p, j], filled)
            matrix[...] = filled
        for copy in copies:
            copy.wait()

    dtype = parts[0].dtype
    results = pl.pallas_call(
        kernel,
        in_specs=[SMEM if whole else HBM]
        + [HBM if whole else VMEM] * part_count + [HBM] * (len(carried) + len(scalars)),
        out_specs=[VMEM] * (picked + len(carried) + len(scalars) + emit),
        out_shape=[jax.ShapeDtypeStruct((listed * tile, LANES), dtype)] * picked
        + [jax.ShapeDtypeStruct(array.shape, array.dtype) for array in carried]
        + [jax.ShapeDtypeStruct((8, LANES), array.dtype) for array in scalars]
        + [jax.ShapeDtypeStruct(matrix_shape, ref_table.dtype)] * emit,
        scratch_shapes=[
            pltpu.SMEM(ref_table.shape, ref_table.dtype),
            pltpu.SemaphoreType.DMA(()),
            pltpu.VMEM((tile if whole else row_count, columns * LANES), dtype),
            pltpu.SemaphoreType.DMA((picked, listed)),
            pltpu.SemaphoreType.DMA((max(len(carried), 1),)),
            pltpu.SMEM((max(len(scalars), 1), 1), jnp.int32),
            pltpu.SemaphoreType.DMA((max(len(scalars), 1),)),
        ],
        compiler_params=PARAMS,
        name="pick_tiles",
    )(ref_table, *parts, *carried, *scalars)
    lists = [results[n : n + slab_count] for n in range(0, picked, slab_count)]
    return lists, results[picked:]


def convolve(arrived, tile_rows, tile_sources, tile_counts, tile_values, row_count, group, chunks):
    slab_count = len(arrived)
    piece, width = arrived[0].shape
    tile = tile_values.shape[2]
    size = row_count // group // chunks
    count_out = group * chunks

    tables = (tile_rows, tile_sources, tile_counts)
    unroll = min(UNROLL, tile_values.shape[1])

    def kernel(*refs):
        values = refs[3]
        pieces = refs[4 : 4 + slab_count]
        outs = refs[4 + slab_count : 4 + slab_count + count_out]
        rows, sources, counts, sems, inputs, total = refs[4 + slab_count + count_out :]
        slab = lax.axis_index("slab")
        _, _, lead = seat(group)
        fetches = [
            pltpu.make_async_copy(refs[n], local_ref, sems.at[n])
            for n, local_ref in enumerate((rows, sources, counts))
        ]
        for fetch in fetches:
            fetch.start()
        for k in range(slab_count):
            start = pl.multiple_of((slab ^ k) * piece, piece)
            inputs[pl.ds(start, piece), :] = pieces[k][...]
        total[...] = jnp.zeros_like(total)
        for fetch in fetches:
            fetch.wait()
        count = counts[0, 0]

        def step(index, carry):
            products = []
            for lane in range(unroll):
                slot = index * unroll + lane
                start = pl.multiple_of(sources[0, slot] * tile, tile)
                product = jnp.dot(
                    values[0, slot],
                    inputs[pl.ds(start, tile), :],
                    preferred_element_type=jnp.float32,
                )
                products.append(jnp.where(slot < count, product, 0.0))
            for lane in range(unroll):
                target = pl.multiple_of(rows[0, index * unroll + lane] * tile, tile)
                total[pl.ds(target, tile), :] += products[lane]
            return carry

        lax.fori_loop(0, (count + unroll - 1) // unroll, step, 0)
        for n in range(count_out):
            start = (lead ^ (n % group)) * (size * chunks) + n // group * size
            rounded = total[pl.ds(pl.multiple_of(start, size), size), :]
            outs[n][...] = rounded.astype(outs[n].dtype)

    dtype = arrived[0].dtype
    results = pl.pallas_call(
        kernel,
        in_specs=[HBM, HBM, HBM, VMEM] + [VMEM] * slab_count,
        out_specs=[VMEM] * count_out,
        out_shape=[jax.ShapeDtypeStruct((size, width), dtype)] * count_out,
        scratch_shapes=[pltpu.SMEM(table.shape, table.dtype) for table in tables]
        + [
            pltpu.SemaphoreType.DMA((3,)),
            pltpu.VMEM((slab_count * piece, width), dtype),
            pltpu.VMEM((row_count, width), jnp.float32),
        ],
        compiler_params=PARAMS,
        name="convolve",
    )(*tables, tile_values, *arrived)
    return [results[n : n + group] for n in range(0, count_out, group)]


def sigmoid(value):
    return 0.5 * jnp.tanh(0.5 * value) + 0.5


def pack(mixed):
    columns, group = len(mixed), len(mixed[0])
    rows, lanes = mixed[0][0].shape
    blocks = [part for column in mixed for part in column]
    size = rows // CHUNKS

    def kernel(*refs):
        _, place, _ = seat(group)
        for n in range(len(blocks)):
            first = n // group * lanes
            for chunk, out in enumerate(refs[len(blocks) :]):
                source = refs[n][chunk * size : (chunk + 1) * size, :]
                out[place ^ (n % group), :, first : first + lanes] = source

    out_shape = jax.ShapeDtypeStruct((group, size, columns * lanes), blocks[0].dtype)
    return list(pl.pallas_call(
        kernel,
        in_specs=[VMEM] * len(blocks),
        out_specs=[VMEM] * CHUNKS,
        out_shape=[out_shape] * CHUNKS,
        compiler_params=PARAMS,
        name="pack",
    )(*blocks))


def pack_chunk(mixed, chunk):
    columns, group = len(mixed), len(mixed[0])
    size = min(column[0].shape[0] for column in mixed)
    lanes = mixed[0][0].shape[1]
    blocks = [part for column in mixed for part in column]

    def kernel(*refs):
        _, place, _ = seat(group)
        for n in range(len(blocks)):
            first = n // group * lanes
            base = chunk * size if blocks[n].shape[0] > size else 0
            source = refs[n][base : base + size, :]
            refs[-1][place ^ (n % group), :, first : first + lanes] = source

    return pl.pallas_call(
        kernel,
        in_specs=[VMEM] * len(blocks),
        out_specs=VMEM,
        out_shape=jax.ShapeDtypeStruct((group, size, columns * lanes), blocks[0].dtype),
        compiler_params=PARAMS,
        name="pack_chunk",
    )(*blocks)


def spread_into(outs, chunks, place, group):
    lanes = outs[0].shape[1]
    for n, out in enumerate(outs):
        first = n // group * lanes
        base = 0
        for chunk in chunks:
            size = chunk.shape[1]
            out[base : base + size, :] = chunk[place ^ (n % group), :, first : first + lanes]
            base += size


def spread(chunks, lanes):
    group, size, units = chunks[0].shape
    count = units // lanes * group

    def kernel(*refs):
        _, place, _ = seat(group)
        spread_into(refs[len(chunks) :], refs[: len(chunks)], place, group)

    results = pl.pallas_call(
        kernel,
        in_specs=[VMEM] * len(chunks),
        out_specs=[VMEM] * count,
        out_shape=[jax.ShapeDtypeStruct((size * len(chunks), lanes), chunks[0].dtype)] * count,
        compiler_params=PARAMS,
        name="spread",
    )(*chunks)
    return [results[n : n + group] for n in range(0, count, group)]


def recur(mixed, layer, w_input, w_hidden, bias, mode, state=None, done=(), keep=(), lanes=0):
    group, size, _ = mixed.shape
    units = w_hidden.shape[1]
    first = state is None
    operands = [mixed] + list(done) + list(keep) + ([] if first else [state])
    outputs = units // lanes * group if lanes else 1

    def kernel(w_in, w_rec, gate_bias, *refs):
        inputs = refs[0]
        earlier = refs[1 : 1 + len(done)]
        kept = refs[1 + len(done) : 1 + len(done) + len(keep)]
        start = refs[len(operands) - 1]
        outs = refs[len(operands) : len(operands) + outputs]
        memory = refs[-1]
        states = refs[-2] if lanes else outs[0]
        half, place, _ = seat(group)

        if keep:

            @pl.when(half != mode)
            def _():
                spread_into(outs, kept, place, group)

        @only(mode, half)
        def _():
            line = gate_bias[layer : layer + 1, :]

            def advance(gates, old, time):
                i, f, g, o = (gates[:, n * units : (n + 1) * units] for n in range(4))
                new = sigmoid(i) * jnp.tanh(g)
                if old is not None:
                    new = sigmoid(f) * old + new
                memory[...] = new
                states[time] = (sigmoid(o) * jnp.tanh(new)).astype(states.dtype)

            def project(time):
                return jnp.dot(inputs[time], w_in[layer], preferred_element_type=jnp.float32) + line

            def step(time, hidden):
                gates = project(time) + jnp.dot(
                    hidden, w_rec[layer], preferred_element_type=jnp.float32
                )
                advance(gates, memory[...], time)

            if first:
                advance(project(0), None, 0)
            else:
                memory[...] = start[1].astype(jnp.float32)
                step(0, start[0])

            def loop(time, carry):
                step(time, states[time - 1])
                return carry

            lax.fori_loop(1, group, loop, 0, unroll=True)
            if lanes:
                spread_into(outs, [*earlier, states], place, group)
            if first:
                last = refs[len(operands) + outputs]
                last[0] = states[group - 1]
                last[1] = memory[...].astype(last.dtype)

    dtype = mixed.dtype
    if lanes:
        out_shape = [jax.ShapeDtypeStruct((size * (1 + len(done)), lanes), dtype)] * outputs
    else:
        out_shape = [jax.ShapeDtypeStruct((group, size, units), dtype)]
    if first:
        out_shape.append(jax.ShapeDtypeStruct((2, size, units), dtype))
    scratch = [pltpu.VMEM((group, size, units), dtype)] if lanes else []
    results = pl.pallas_call(
        kernel,
        in_specs=[VMEM] * (3 + len(operands)),
        out_specs=[VMEM] * len(out_shape),
        out_shape=out_shape,
        scratch_shapes=scratch + [pltpu.VMEM((size, units), jnp.float32)],
        compiler_params=PARAMS,
        name="recur",
    )(w_input, w_hidden, bias, *operands)
    if lanes:
        return [results[n : n + group] for n in range(0, outputs, group)]
    return results if first else results[0]


def assemble(parts):
    group = len(parts[0])
    size, width = parts[0][0].shape
    part_rows = size * len(parts)
    count = len(parts) * group

    def kernel(*refs):
        out, sems = refs[-2:]
        _, _, lead = seat(group)
        copies = []
        for n in range(count):
            start = (lead ^ (n % group)) * part_rows + n // group * size
            target = out.at[0, pl.ds(pl.multiple_of(start, size), size)]
            copies.append(pltpu.make_async_copy(refs[n], target, sems.at[n]))
        for copy in copies:
            copy.start()
        for copy in copies:
            copy.wait()

    return pl.pallas_call(
        kernel,
        in_specs=[VMEM] * count,
        out_specs=HBM,
        out_shape=jax.ShapeDtypeStruct((1, group * part_rows, width), parts[0][0].dtype),
        scratch_shapes=[pltpu.SemaphoreType.DMA((count,))],
        compiler_params=PARAMS,
        name="assemble",
    )(*(part for chunk in parts for part in chunk))


def send(array, target, lower_only=False):
    slab_count = lax.axis_size("slab")
    times = lax.axis_size("tm")
    pairs = []
    for time in range(times // 2 if lower_only else times):
        for slab in range(slab_count):
            to_time, to_slab = target(time, slab)
            pairs.append((time * slab_count + slab, to_time * slab_count + to_slab))
    return lax.ppermute(array, AXES, pairs)


def swap_slabs(arrays):
    got = list(arrays)
    for k in range(len(arrays) - 1, 0, -1):
        got[k] = send(arrays[k], lambda time, slab: (time, slab ^ k))
    return got


def swap_times(arrays):
    got = list(arrays)
    for k in range(len(arrays) - 1, 0, -1):
        got[k] = send(arrays[k], lambda time, slab: (time ^ k, slab))
    return got


def hand_over(last, group):
    flip = mirror(group)
    return send(last, lambda time, slab: (group + (time ^ flip), slab), lower_only=True)


def local(
    features, ref_lists, tile_rows, tile_sources, tile_counts, tile_values, w_input, w_hidden, bias
):
    row_count = features.shape[1]
    tile = tile_values.shape[2]
    slab_count = lax.axis_size("slab")
    layers = w_input.shape[0]
    group = lax.axis_size("tm") // 2
    half = lax.axis_index("tm") // group

    def pick(parts, table, *carried):
        length = ref_lists.shape[2] // slab_count
        return pick_tiles(parts, table, length, slab_count, row_count, tile, group, *carried)

    def mix(listed, live, chunks=1):
        arrived = swap_slabs(listed)
        mixed = convolve(
            arrived, tile_rows, tile_sources, live, tile_values, row_count, group, chunks
        )
        got = []
        for part in mixed:
            got.append(swap_times(part))
        return got if chunks > 1 else got[0]

    def back_and_mix(hidden):
        return pack([mix(pick(swap_times(column), table)[0][0], counts) for column in hidden])

    def run(mixed, layer, mode, *rest):
        return recur(mixed, layer, w_input, w_hidden, gate_bias, mode, *rest)

    def run_lower(mixed, layer):
        chunks, handed = [], []
        for part in mixed:
            states, last = run(part, layer, LOWER)
            handed.append(hand_over(last, group))
            chunks.append(states)
        return chunks, handed

    def run_upper(mixed, layer, states):
        return [run(part, layer, UPPER, state) for part, state in zip(mixed[:-1], states)]

    listed, (gate_bias, counts, table) = pick([features[0]], ref_lists, (bias,), (tile_counts,))
    *listed, last = listed
    early = [mix(column, tile_counts) for column in listed]
    upper_mixed = [
        pack_chunk([*early, part], chunk) for chunk, part in enumerate(mix(last, tile_counts, CHUNKS))
    ]
    hidden, handed = run_lower(upper_mixed, 0)
    for layer in range(1, layers):

        def lower_layer(hidden):
            return back_and_mix(spread(hidden, LANES)), half + 1

        def upper_layer(mixed, done, state):
            return back_and_mix(run(mixed[-1], layer - 1, BOTH, state, done, (), LANES))

        lower_mixed, turn = lax.cond(
            half == LOWER, lower_layer, lambda hidden: (hidden, half), hidden
        )
        hidden, following = run_lower(lower_mixed, layer)
        done = run_upper(upper_mixed, layer - 1, handed)
        upper_mixed = lax.cond(
            half == turn,
            upper_layer,
            lambda mixed, done, state: mixed,
            upper_mixed,
            done,
            handed[-1],
        )
        handed = following
    units = w_hidden.shape[1]
    parts = []
    for number, (part, state) in enumerate(zip(upper_mixed, handed)):
        (states,) = run(part, layers - 1, UPPER, state, (), hidden[number : number + 1], units)
        parts.append(swap_times(states))
    return assemble(parts)


def solution(mesh):
    in_specs = (
        P("tm", "slab", None),
        P("tm", None, None),
        P("tm", "slab"),
        P("tm", "slab"),
        P("tm", "slab"),
        P("tm", "slab", None, None),
        P(),
        P(),
        P(),
    )
    out_specs = P("tm", "slab", None)
    return jax.shard_map(local, mesh=mesh, in_specs=in_specs, out_specs=out_specs, check_vma=False)
```
